256 devices in a mesh: dp: 16 (over z, x_hi), section: 4 (over y), tensor: 4 (over x_lo, core).
Axes of the slice: x: 4 (x_hi: 2, x_lo: 2; x = x_hi * 2 + x_lo), y: 4, z: 8, core: 2. Of those that a mesh axis runs over, the one named last changes fastest.
Arguments:
- block_in: bfloat16 [512, 16, 512], P('dp', None, 'tensor'), may hold values from -128 to 128
- weights: bfloat16 [12, 16, 512, 8192], P('section', None, 'tensor', 'dp'), may hold values from -0.0625 to 0.0625
- gains: float32 [12, 16, 512], P('section', None, 'tensor'), may hold values from 0.1 to 1.9
- layer_counts: int32 [4], replicated, may hold values from 1 to 3, 8 in all
Outputs:
- block_out: bfloat16 [512, 16, 512], P('dp', None, 'tensor')
- gram_in: float32 [16, 512, 16, 512], P(None, 'tensor', 'dp', 'section')
- gram_cross: float32 [16, 512, 16, 512], P(None, 'tensor', 'dp', 'section')
The draws below stay inside these ranges and needn't reach their ends.
Inputs may be any that keep to these rules, and one draw needn't show every extreme that they name: `layer_counts`: each entry is 1 to 3, they sum to 8, and the largest is exactly 3.
All inputs are finite; a program needn't handle non-finite values.
Results may differ from the reference program's by a relative error of at most 0.0093.
Values may be sent and summed in bfloat16 or wider, within the bound.
No kernel may reach another device: no remote copies, remote signals or barrier semaphores. Data moves between devices by JAX's collectives and lax.ppermute only.
A program may use at most 64 MiB of HBM per device.

```python
import math
import jax
import jax.numpy as jnp
import numpy as np
from jax import lax

D = 8192
SLOTS = 3
LAYERS = 8
TOKENS = 512
NBLK = 16
BLKW = 512
QUART = 128
N_SECTION = 4


def draw_block_in(key, part):
    first, second = jax.random.split(jax.random.fold_in(key, 11), 2)
    position = jnp.arange(BLKW) // QUART
    ramp_up = 3.0 ** (position.astype(jnp.float32) / max(BLKW // QUART - 1, 1))
    ramp_up = ramp_up.reshape(1, 1, BLKW)
    jitter = jnp.exp(jax.random.uniform(second, (1, NBLK, BLKW), minval=0.0, maxval=math.log(2.0)))
    values = jnp.clip(jax.random.normal(first, (TOKENS, NBLK, BLKW)), -4.0, 4.0) * ramp_up * jitter
    return values.astype(jnp.float32).astype(jnp.bfloat16)


def steps_of(rng, extent, pieces, least, largest):
    factor_of, own = 1.0, jax.random.fold_in(rng, 6)
    for axis_at, blocks in pieces:
        draws = jnp.exp(jax.random.uniform(jax.random.fold_in(own, axis_at), (blocks,), jnp.float32, least / len(pieces), largest / len(pieces)))
        factor_of = factor_of * jnp.repeat(draws, extent[axis_at] // blocks).reshape([-1 if axis == axis_at else 1 for axis in range(len(extent))])
    return factor_of


def profile(count, total, limit, lean):
    portions = [(1 << 20) // math.isqrt(standing ** lean) + 1 for standing in range(2, count + 1)]
    surplus, holding = total - limit - (count - 1), [1] * (count - 1)
    while surplus > 0:
        candidates = [i for i in range(count - 1) if holding[i] < limit]
        whole, budget = sum([portions[i] for i in candidates]), surplus
        for i in candidates:
            more = min(limit - holding[i], max(1, budget * portions[i] // whole), surplus)
            holding[i] = holding[i] + more
            surplus = surplus - more
    return np.array([limit] + holding)


def ragged_sizes(rng, count, total, reach, slope):
    if count == 2:
        one = jax.random.randint(rng, (), max(1, total - reach), min(reach, total - 1) + 1)
        return jnp.stack([one, total - one])
    tallies = jnp.asarray(profile(count, total, reach, slope), jnp.int32)
    couples = (count - 1) // 2
    source_of, sink = tallies[1:1 + 2 * couples:2], tallies[2:2 + 2 * couples:2]
    room = jnp.minimum(source_of - 1, reach - sink)
    passed = jax.random.randint(jax.random.fold_in(rng, 1), (couples,), 0, 1 << 20) % (room + 1)
    tallies = tallies.at[1:1 + 2 * couples:2].set(source_of - passed).at[2:2 + 2 * couples:2].set(sink + passed)
    return tallies[jax.random.permutation(jax.random.fold_in(rng, 2), count)]


def gaussian(stream_key, shape, deviation, reach, cuts=(), kind=jnp.bfloat16):
    gain = steps_of(stream_key, shape, cuts, -0.22, 0.18) if cuts else 1.0
    array = jax.random.normal(stream_key, shape, jnp.float32) * deviation * gain
    return jnp.minimum(jnp.maximum(array, -reach), reach).astype(kind)


def setup_inputs(seed: int = 0) -> dict:
    keys = jax.random.split(jax.random.key(seed), 5)
    return {
        "block_in": draw_block_in(jax.random.fold_in(keys[4], 71), 0),
        "weights": gaussian(keys[1], (N_SECTION * SLOTS, NBLK, BLKW, D), D ** -0.5, 0.0625, ((0, 4), (2, 4), (3, 16))),
        "gains": jnp.clip(1.0 + 0.18 * jax.random.normal(keys[2], (N_SECTION * SLOTS, NBLK, BLKW), jnp.float32), 0.1, 1.9),
        "layer_counts": ragged_sizes(keys[3], N_SECTION, LAYERS, SLOTS, 0).astype(jnp.int32),
    }


EPSILON = 1e-05

def run_layer(hidden, matrix, gain_row):
    wide_rows = hidden.astype(jnp.float32)
    mean_square = lax.optimization_barrier(jnp.sum(wide_rows * wide_rows, axis=1, keepdims=True)) / D
    normed = (wide_rows * lax.rsqrt(mean_square + EPSILON) * gain_row[None, :]).astype(jnp.bfloat16)
    update = jnp.dot(normed, matrix, preferred_element_type=jnp.float32).astype(jnp.bfloat16)
    update = lax.optimization_barrier(update)
    return (wide_rows + update.astype(jnp.float32)).astype(jnp.bfloat16)

def reference(block_in, weights, gains, layer_counts):
    block_rows = block_in.reshape(TOKENS, D)
    hidden = block_rows
    for segment_pos in range(N_SECTION):
        for slot_id in range(SLOTS):
            slot_flat = segment_pos * SLOTS + slot_id
            matrix = weights[slot_flat].reshape(D, D)
            gain_row = gains[slot_flat].reshape(D)
            hidden = lax.cond(slot_id < layer_counts[segment_pos], lambda value, mat=matrix, gvec=gain_row: run_layer(value, mat, gvec), lambda value: value, hidden)
    gram_in = jnp.dot(block_rows.T, block_rows, preferred_element_type=jnp.float32) / TOKENS
    gram_cross = jnp.dot(block_rows.T, hidden, preferred_element_type=jnp.float32) / TOKENS
    return (hidden.reshape(TOKENS, NBLK, BLKW), gram_in.reshape(NBLK, BLKW, NBLK, BLKW), gram_cross.reshape(NBLK, BLKW, NBLK, BLKW))
```

```python
import functools
import jax
import jax.numpy as jnp
import numpy as np
from jax import lax
from jax.experimental import pallas as pl
from jax.experimental.pallas import tpu as pltpu
from jax.sharding import Mesh, PartitionSpec as P

D = 8192
SLOTS = 3
LAYERS = 8
TOKENS = 512
NBLK = 16
LANE = 128
NZ = 8
NY = 4
EPSILON = 1e-05
TAIL = 16
GROUPS = TOKENS // LANE
AXES = ("z", "xh", "y", "xl", "c")
IN_VMEM = pl.BlockSpec(memory_space=pltpu.VMEM)
IN_SMEM = pl.BlockSpec(memory_space=pltpu.SMEM)
IN_PLACE = pl.BlockSpec(memory_space=pl.ANY)


def send(array, axes, sizes, route):
    pairs = []
    for source in np.ndindex(*sizes):
        target = route(*source)
        if target is not None:
            pairs.append((int(np.ravel_multi_index(source, sizes)), int(np.ravel_multi_index(target, sizes))))
    return lax.ppermute(array, axes, pairs)


def swap_roles(array):
    return send(array, ("xh", "c"), (2, 2), lambda xh, c: (c, xh))


def other_core(array):
    return send(array, ("c",), (2,), lambda c: (1 - c,))


def round_z(array):
    return send(array, ("z", "c"), (NZ, 2), lambda z, c: ((z + 1 - 2 * c) % NZ, c))


def round_x(array, step):
    def route(xh, xl):
        place = (2 * xh + xl + step) % 4
        return place // 2, place % 2

    return send(array, ("xh", "xl"), (2, 2), route)


def gather(block):
    rows = block.shape[0]
    other = other_core(block)
    held = jnp.concatenate([block, other], axis=0)
    parts = [block, other]
    for _ in range(3):
        held = round_z(held)
        parts += [held, other_core(held)]
    held = round_z(held[:rows])
    return parts + [held, other_core(held)]


def block_table():
    table = np.zeros((NZ, 2, 2, 2, 24), np.int32)
    for z, xh, xl, c in np.ndindex(NZ, 2, 2, 2):
        away = -1 if c == 0 else 1
        order = [(z, c), (z, 1 - c)]
        for r in range(1, 4):
            order += [(z + away * r, c), (z + away * r, 1 - c)]
            order += [(z - away * r, 1 - c), (z - away * r, c)]
        order += [(z + 4, c), (z + 4, 1 - c)]
        row = [2 * (at % NZ) + core for at, core in order]
        for step in range(4):
            place = (2 * xh + xl + step) % 4
            row.append(2 * (place % 2) + place // 2)
        table[z, xh, xl, c, : len(row)] = row
    return table.reshape(-1, 24)


def halves(refs):
    rows = refs[0].shape[0]
    pieces = []
    for ref in refs:
        pieces += [ref[k * rows : (k + 1) * rows, :] for k in range(ref.shape[0] // rows)]
    return pieces


def assemble_body(table, *refs):
    parts, whole = refs[:-1], refs[-1]
    rows = TOKENS // NBLK
    for k, piece in enumerate(halves(parts)):
        at = pl.multiple_of(table[k] * rows, rows)
        for b in range(NBLK):
            whole[b, pl.ds(at, rows), :] = piece[b * rows : (b + 1) * rows, :]


def assemble(table, parts):
    return pl.pallas_call(
        assemble_body,
        out_shape=jax.ShapeDtypeStruct((NBLK, TOKENS, LANE), jnp.bfloat16),
        in_specs=[IN_SMEM] + [IN_VMEM] * len(parts),
        out_specs=IN_VMEM,
        name="assemble",
        cost_estimate=pl.CostEstimate(flops=0, bytes_accessed=4 << 20, transcendentals=0),
        compiler_params=pltpu.CompilerParams(vmem_limit_bytes=24 << 20),
    )(table, *parts)


def in_three(value):
    first = value.astype(jnp.bfloat16)
    rest = value - first.astype(jnp.float32)
    second = rest.astype(jnp.bfloat16)
    third = (rest - second.astype(jnp.float32)).astype(jnp.bfloat16)
    return [first, second, third]


def project_body(layer, n_parts, n_weights, *refs):
    table, slots = refs[:2]
    parts = refs[2 : 2 + n_parts]
    gains = refs[2 + n_parts]
    weights = refs[3 + n_parts : 3 + n_parts + n_weights]
    outs = refs[3 + n_parts + n_weights :]
    sends, own, own_squares = outs[:3], outs[3], outs[4]
    rows, matrix, product, arrived = outs[5:]
    slot = slots[layer]
    for k, weight in enumerate(weights):
        last = k == n_weights - 1
        chosen = slot >= k if last else slot == k

        @pl.when(chosen)
        def _(weight=weight):
            pltpu.make_async_copy(weight, matrix, arrived).start()

    squares = jnp.zeros((TOKENS, LANE), jnp.float32)
    if n_parts == 1:
        pieces = [(b, parts[0][b]) for b in range(NBLK)]
    else:
        pieces = [(table[k], piece) for k, piece in enumerate(halves(parts))]
    for b, piece in pieces:
        wide = piece.astype(jnp.float32)
        squares = squares + wide * wide
        scaled = (wide * gains[slot * NBLK + b]).astype(jnp.bfloat16)
        rows[:, pl.ds(pl.multiple_of(b * LANE, LANE), LANE)] = scaled
    sums = jnp.concatenate(
        [jnp.sum(squares[a * LANE : (a + 1) * LANE].T, axis=0, keepdims=True) for a in range(GROUPS)], axis=0
    )
    own_squares[...] = sums
    tail = jnp.concatenate(in_three(sums) + [jnp.zeros((TAIL - 3 * GROUPS, LANE), jnp.bfloat16)], axis=0)
    pltpu.make_async_copy(weights[0], matrix, arrived).wait()
    for pair in range(2):
        total = jnp.dot(rows[...], matrix[:, pair * 256 : (pair + 1) * 256], preferred_element_type=jnp.float32)
        product[2 * pair] = total[:, :LANE]
        product[2 * pair + 1] = total[:, LANE:]
    own[...] = product[table[16]]
    for step in range(1, 4):
        sends[step - 1][0:TOKENS, :] = product[table[16 + step]].astype(jnp.bfloat16)
        sends[step - 1][TOKENS : TOKENS + TAIL, :] = tail


def project(layer, table, slots, parts, gains, weights):
    outs = [jax.ShapeDtypeStruct((TOKENS + TAIL, LANE), jnp.bfloat16)] * 3
    outs += [jax.ShapeDtypeStruct((TOKENS, LANE), jnp.float32), jax.ShapeDtypeStruct((GROUPS, LANE), jnp.float32)]
    return pl.pallas_call(
        functools.partial(project_body, layer, len(parts), len(weights)),
        out_shape=outs,
        in_specs=[IN_SMEM] * 2 + [IN_VMEM] * (len(parts) + 1) + [IN_PLACE] * len(weights),
        out_specs=[IN_VMEM] * 5,
        scratch_shapes=[
            pltpu.VMEM((TOKENS, NBLK * LANE), jnp.bfloat16),
            pltpu.VMEM((NBLK * LANE, 512), jnp.bfloat16),
            pltpu.VMEM((4, TOKENS, LANE), jnp.float32),
            pltpu.SemaphoreType.DMA,
        ],
        name="project",
        cost_estimate=pl.CostEstimate(flops=2 * TOKENS * 2048 * 512, bytes_accessed=6 << 20, transcendentals=0),
        compiler_params=pltpu.CompilerParams(vmem_limit_bytes=32 << 20),
    )(table, slots, *parts, gains, *weights)


def update_body(current, own, own_squares, *refs):
    arrived, result = refs[:3], refs[3]
    total, squares = own[...], own_squares[...]
    for ref in arrived:
        total = total + ref[0:TOKENS, :].astype(jnp.float32)
        tail = ref[TOKENS : TOKENS + TAIL, :].astype(jnp.float32)
        squares = squares + (tail[0:GROUPS] + tail[GROUPS : 2 * GROUPS] + tail[2 * GROUPS : 3 * GROUPS])
    scale = lax.rsqrt(squares * (1.0 / D) + EPSILON)
    column = jnp.concatenate(
        [jnp.broadcast_to(scale[a : a + 1], (LANE, LANE)).T for a in range(GROUPS)], axis=0
    )
    step = (total * column).astype(jnp.bfloat16).astype(jnp.float32)
    result[...] = (current[...].astype(jnp.float32) + step).astype(jnp.bfloat16)


def update(current, own, own_squares, arrived):
    return pl.pallas_call(
        update_body,
        out_shape=jax.ShapeDtypeStruct((TOKENS, LANE), jnp.bfloat16),
        in_specs=[IN_VMEM] * 6,
        out_specs=IN_VMEM,
        name="update",
        cost_estimate=pl.CostEstimate(flops=20 * TOKENS * LANE, bytes_accessed=1 << 20, transcendentals=512),
        compiler_params=pltpu.CompilerParams(vmem_limit_bytes=16 << 20),
    )(current, own, own_squares, *arrived)


def gram_body(rows, columns, result):
    right = columns[...]
    for b in range(NBLK):
        total = lax.dot_general(rows[b], right, (((0,), (0,)), ((), ())), preferred_element_type=jnp.float32)
        result[b] = total * (1.0 / TOKENS)


def gram(rows, columns):
    return pl.pallas_call(
        gram_body,
        out_shape=jax.ShapeDtypeStruct((NBLK, LANE, LANE), jnp.float32),
        in_specs=[IN_VMEM] * 2,
        out_specs=IN_VMEM,
        name="gram",
        cost_estimate=pl.CostEstimate(flops=2 * TOKENS * 2048 * LANE, bytes_accessed=3 << 20, transcendentals=0),
        compiler_params=pltpu.CompilerParams(vmem_limit_bytes=16 << 20),
    )(rows, columns)


def quarter_of_section(block):
    own_quarter = 2 * lax.axis_index("xl") + lax.axis_index("c") == lax.axis_index("y")
    across = send(
        block, ("y", "xl", "c"), (NY, 2, 2), lambda y, xl, c: (y, 1 - xl, c) if 2 * xl + c == y else None
    )
    here = jnp.where(own_quarter, block, across)
    beside = send(here, ("y", "xl", "c"), (NY, 2, 2), lambda y, xl, c: (y, xl, 1 - c) if c == y % 2 else None)
    return jnp.where(lax.axis_index("c") == lax.axis_index("y") % 2, here, beside)


def local(block_in, weights, gains, layer_counts):
    section = lax.axis_index("y")
    sections = jnp.arange(NY, dtype=jnp.int32)
    start = jnp.sum(jnp.where(sections < section, layer_counts, 0))
    layers = jnp.arange(LAYERS, dtype=jnp.int32)
    slots = jnp.clip(layers - start, 0, SLOTS - 1)
    ends = jnp.sum(jnp.where(sections[None, :] <= sections[:3, None], layer_counts[None, :], 0), axis=1)
    hops = jnp.any(ends[:, None] == layers[None, :] + 1, axis=0)
    table = lax.dynamic_index_in_dim(
        jnp.asarray(block_table()), lax.axis_index(("z", "xh", "xl", "c")), 0, keepdims=False
    )

    gains = swap_roles(gains.reshape(SLOTS * NBLK, 1, LANE))
    tiles = [swap_roles(weights[k].reshape(NBLK * LANE, 512)) for k in range(SLOTS)]

    by_block = block_in.transpose(1, 0, 2).reshape(TOKENS, LANE)
    whole = assemble(table, gather(swap_roles(by_block)))
    current = lax.dynamic_index_in_dim(
        whole, 2 * lax.axis_index("z") + lax.axis_index("c"), 0, keepdims=False
    )
    parts = [whole]
    for layer in range(LAYERS):
        if layer:
            parts = gather(current)
        outs = project(layer, table, slots, parts, gains, tiles[: layer + 1])
        arrived = [round_x(outs[k], k + 1) for k in range(3)]
        current = update(current, outs[3], outs[4], arrived)
        if layer < LAYERS - 1:
            current = lax.cond(
                hops[layer],
                lambda v: send(v, ("y",), (NY,), lambda y: (y + 1,) if y < NY - 1 else None),
                lambda v: v,
                current,
            )

    rows = swap_roles(whole)
    x0 = lax.dynamic_index_in_dim(rows, 2 * lax.axis_index("z") + lax.axis_index("xh"), 0, keepdims=False)
    gram_in = gram(rows, quarter_of_section(x0))

    copies = [
        send(
            current,
            ("xh", "y", "xl", "c"),
            (2, NY, 2, 2),
            lambda xh, y, xl, c, plane=plane: (c, plane, xl, xh) if y == NY - 1 else None,
        )
        for plane in range(NY)
    ]
    final = copies[0]
    for plane in range(1, NY):
        final = jnp.where(section == plane, copies[plane], final)
    block_out = lax.all_to_all(final.reshape(NBLK, TOKENS // NBLK, LANE), ("z", "xh"), 0, 0, tiled=True)
    gram_cross = gram(rows, quarter_of_section(final))
    shape = (NBLK, LANE, 1, LANE)
    return block_out.transpose(1, 0, 2), gram_in.reshape(shape), gram_cross.reshape(shape)


def solution(mesh):
    finer = Mesh(mesh.devices.reshape(NZ, 2, NY, 2, 2), AXES)
    dp, section, tensor = ("z", "xh"), "y", ("xl", "c")
    return jax.shard_map(
        local,
        mesh=finer,
        in_specs=(P(dp, None, tensor), P(section, None, tensor, dp), P(section, None, tensor), P()),
        out_specs=(P(dp, None, tensor), P(None, tensor, dp, section), P(None, tensor, dp, section)),
        check_vma=False,
    )
```

```python
import functools
import jax
import jax.numpy as jnp
import numpy as np
from jax import lax
from jax.experimental import pallas as pl
from jax.experimental.pallas import tpu as pltpu
from jax.sharding import Mesh, PartitionSpec as P

D = 8192
SLOTS = 3
LAYERS = 8
TOKENS = 512
NBLK = 16
LANE = 128
NZ = 8
NY = 4
EPSILON = 1e-05
TAIL = 16
GROUPS = TOKENS // LANE
EARLY = 10
LATE = NBLK - EARLY
AXES = ("z", "xh", "y", "xl", "c")
IN_VMEM = pl.BlockSpec(memory_space=pltpu.VMEM)
IN_SMEM = pl.BlockSpec(memory_space=pltpu.SMEM)
IN_PLACE = pl.BlockSpec(memory_space=pltpu.HBM)


def send(array, axes, sizes, route):
    pairs = []
    for source in np.ndindex(*sizes):
        target = route(*source)
        if target is not None:
            pairs.append((int(np.ravel_multi_index(source, sizes)), int(np.ravel_multi_index(target, sizes))))
    return lax.ppermute(array, axes, pairs)


def swap_roles(array):
    return send(array, ("xh", "c"), (2, 2), lambda xh, c: (c, xh) if xh != c else None)


def other_core(array):
    return send(array, ("c",), (2,), lambda c: (1 - c,))


def along_z(array, distance):
    return send(array, ("z", "c"), (NZ, 2), lambda z, c: ((z + distance * (1 - 2 * c)) % NZ, c))


def along_x(array, step):
    def route(xh, xl):
        place = (2 * xh + xl + step) % 4
        return place // 2, place % 2

    return send(array, ("xh", "xl"), (2, 2), route)


def first_round(block):
    other = other_core(block)
    chip = jnp.concatenate([block, other], axis=0)
    near, far = along_z(chip, 1), along_z(chip, 2)
    return [block, other, near, other_core(near), far, other_core(far)]


def second_round(parts, before=None):
    block, far = parts[0], parts[4]
    third, fourth = along_z(far, 1), along_z(far[: block.shape[0]], 2)
    if before is not None:
        third, fourth, _ = lax.optimization_barrier((third, fourth, before))
    return [third, other_core(third), fourth, other_core(fourth)]


def block_table():
    table = np.zeros((NZ, 2, 2, 2, 24), np.int32)
    for z, xh, xl, c in np.ndindex(NZ, 2, 2, 2):
        away = -1 if c == 0 else 1
        order = [(z, c), (z, 1 - c)]
        for r in range(1, 4):
            order += [(z + away * r, c), (z + away * r, 1 - c)]
            order += [(z - away * r, 1 - c), (z - away * r, c)]
        order += [(z + 4, c), (z + 4, 1 - c)]
        row = [2 * (at % NZ) + core for at, core in order]
        for step in range(4):
            place = (2 * xh + xl + step) % 4
            row.append(2 * (place % 2) + place // 2)
        row.append(int(xh == c))
        table[z, xh, xl, c, : len(row)] = row
    return table.reshape(-1, 24)


def pieces_of(refs):
    rows = min(ref.shape[0] for ref in refs)
    pieces = []
    for ref in refs:
        pieces += [ref[k * rows : (k + 1) * rows, :] for k in range(ref.shape[0] // rows)]
    return pieces


def assemble_body(table, *refs):
    parts, whole = refs[:-1], refs[-1]
    rows = TOKENS // NBLK
    for k, piece in enumerate(pieces_of(parts)):
        at = pl.multiple_of(table[k] * rows, rows)
        for b in range(NBLK):
            whole[b, pl.ds(at, rows), :] = piece[b * rows : (b + 1) * rows, :]


def assemble(table, parts):
    return pl.pallas_call(
        assemble_body,
        out_shape=jax.ShapeDtypeStruct((NBLK, TOKENS, LANE), jnp.bfloat16),
        in_specs=[IN_SMEM] + [IN_VMEM] * len(parts),
        out_specs=IN_VMEM,
        name="assemble",
        cost_estimate=pl.CostEstimate(flops=0, bytes_accessed=4 << 20, transcendentals=0),
        compiler_params=pltpu.CompilerParams(vmem_limit_bytes=24 << 20),
    )(table, *parts)


def in_three(value):
    first = value.astype(jnp.bfloat16)
    rest = value - first.astype(jnp.float32)
    second = rest.astype(jnp.bfloat16)
    third = (rest - second.astype(jnp.float32)).astype(jnp.bfloat16)
    return [first, second, third]


def scale_rows(pieces, gains, at, rows):
    squares = jnp.zeros((TOKENS, LANE), jnp.float32)
    for k, piece in enumerate(pieces):
        wide = piece.astype(jnp.float32)
        squares = squares + wide * wide
        rows[:, k * LANE : (k + 1) * LANE] = (wide * gains[at[k]]).astype(jnp.bfloat16)
    return squares


def begin_body(layer, n_parts, n_tiles, *refs):
    table, slots = refs[:2]
    parts, gains = refs[2 : 2 + n_parts], refs[2 + n_parts]
    tiles = refs[3 + n_parts : 3 + n_parts + n_tiles]
    partial, squares, later, rows, matrix, arrived = refs[3 + n_parts + n_tiles :]
    slot = slots[layer]
    order = list(range(NBLK)) if n_parts == 1 else [table[k] for k in range(NBLK)]

    def fetch(source):
        for k, b in enumerate(order):
            into = matrix if k < EARLY else later
            at = k if k < EARLY else k - EARLY
            pltpu.make_async_copy(
                source.at[b], into.at[pl.ds(at * LANE, LANE), :], arrived.at[int(k >= EARLY)]
            ).start()

    for k, tile in enumerate(tiles):

        @pl.when(slot >= k if k == n_tiles - 1 else slot == k)
        def _(tile=tile):
            fetch(tile)

    pieces = [parts[0][b] for b in range(EARLY)] if n_parts == 1 else pieces_of(parts)
    squares[...] = scale_rows(pieces, gains, [slot * NBLK + b for b in order[:EARLY]], rows)
    pltpu.make_async_copy(matrix, matrix, arrived.at[0]).wait()
    for pair in range(2):
        total = jnp.dot(rows[...], matrix[:, pair * 256 : (pair + 1) * 256], preferred_element_type=jnp.float32)
        partial[2 * pair] = total[:, :LANE]
        partial[2 * pair + 1] = total[:, LANE:]
    pltpu.make_async_copy(later, later, arrived.at[1]).wait()


def begin(layer, table, slots, parts, gains, tiles):
    return pl.pallas_call(
        functools.partial(begin_body, layer, len(parts), len(tiles)),
        out_shape=[
            jax.ShapeDtypeStruct((4, TOKENS, LANE), jnp.float32),
            jax.ShapeDtypeStruct((TOKENS, LANE), jnp.float32),
            jax.ShapeDtypeStruct((LATE * LANE, 512), jnp.bfloat16),
        ],
        in_specs=[IN_SMEM] * 2 + [IN_VMEM] * (len(parts) + 1) + [IN_PLACE] * len(tiles),
        out_specs=[IN_VMEM] * 3,
        scratch_shapes=[
            pltpu.VMEM((TOKENS, EARLY * LANE), jnp.bfloat16),
            pltpu.VMEM((EARLY * LANE, 512), jnp.bfloat16),
            pltpu.SemaphoreType.DMA((2,)),
        ],
        name="begin",
        cost_estimate=pl.CostEstimate(flops=2 * TOKENS * 1280 * 512, bytes_accessed=5 << 20, transcendentals=0),
        compiler_params=pltpu.CompilerParams(vmem_limit_bytes=24 << 20),
    )(table, slots, *parts, gains, *tiles)


def finish_body(layer, n_parts, *refs):
    table, slots = refs[:2]
    parts = refs[2 : 2 + n_parts]
    gains, partial, squares, later = refs[2 + n_parts : 6 + n_parts]
    sends, own, own_squares, rows, product = refs[6 + n_parts : 9 + n_parts], *refs[9 + n_parts :]
    slot = slots[layer]
    if n_parts == 1:
        pieces, order = [parts[0][b] for b in range(EARLY, NBLK)], range(EARLY, NBLK)
    else:
        pieces, order = pieces_of(parts), [table[k] for k in range(EARLY, NBLK)]
    total = squares[...] + scale_rows(pieces, gains, [slot * NBLK + b for b in order], rows)
    for pair in range(2):
        both = jnp.dot(rows[...], later[:, pair * 256 : (pair + 1) * 256], preferred_element_type=jnp.float32)
        product[2 * pair] = both[:, :LANE]
        product[2 * pair + 1] = both[:, LANE:]
    sums = jnp.concatenate(
        [jnp.sum(total[a * LANE : (a + 1) * LANE].T, axis=0, keepdims=True) for a in range(GROUPS)], axis=0
    )
    own_squares[...] = sums
    tail = jnp.concatenate(in_three(sums) + [jnp.zeros((TAIL - 3 * GROUPS, LANE), jnp.bfloat16)], axis=0)
    own[...] = product[table[16]] + partial[table[16]]
    for step in range(1, 4):
        quarter = table[16 + step]
        sends[step - 1][0:TOKENS, :] = (product[quarter] + partial[quarter]).astype(jnp.bfloat16)
        sends[step - 1][TOKENS : TOKENS + TAIL, :] = tail


def finish(layer, table, slots, parts, gains, begun):
    outs = [jax.ShapeDtypeStruct((TOKENS + TAIL, LANE), jnp.bfloat16)] * 3
    outs += [jax.ShapeDtypeStruct((TOKENS, LANE), jnp.float32), jax.ShapeDtypeStruct((GROUPS, LANE), jnp.float32)]
    return pl.pallas_call(
        functools.partial(finish_body, layer, len(parts)),
        out_shape=outs,
        in_specs=[IN_SMEM] * 2 + [IN_VMEM] * (len(parts) + 4),
        out_specs=[IN_VMEM] * 5,
        scratch_shapes=[
            pltpu.VMEM((TOKENS, LATE * LANE), jnp.bfloat16),
            pltpu.VMEM((4, TOKENS, LANE), jnp.float32),
        ],
        name="finish",
        cost_estimate=pl.CostEstimate(flops=2 * TOKENS * 768 * 512, bytes_accessed=5 << 20, transcendentals=0),
        compiler_params=pltpu.CompilerParams(vmem_limit_bytes=24 << 20),
    )(table, slots, *parts, gains, *begun)


def update_body(current, own, own_squares, *refs):
    arrived, result = refs[:3], refs[3]
    total, squares = own[...], own_squares[...]
    for ref in arrived:
        total = total + ref[0:TOKENS, :].astype(jnp.float32)
        tail = ref[TOKENS : TOKENS + TAIL, :].astype(jnp.float32)
        squares = squares + (tail[0:GROUPS] + tail[GROUPS : 2 * GROUPS] + tail[2 * GROUPS : 3 * GROUPS])
    scale = lax.rsqrt(squares * (1.0 / D) + EPSILON)
    column = jnp.concatenate(
        [jnp.broadcast_to(scale[a : a + 1], (LANE, LANE)).T for a in range(GROUPS)], axis=0
    )
    step = (total * column).astype(jnp.bfloat16).astype(jnp.float32)
    result[...] = (current[...].astype(jnp.float32) + step).astype(jnp.bfloat16)


def update(current, own, own_squares, arrived):
    return pl.pallas_call(
        update_body,
        out_shape=jax.ShapeDtypeStruct((TOKENS, LANE), jnp.bfloat16),
        in_specs=[IN_VMEM] * 6,
        out_specs=IN_VMEM,
        name="update",
        cost_estimate=pl.CostEstimate(flops=20 * TOKENS * LANE, bytes_accessed=1 << 20, transcendentals=512),
        compiler_params=pltpu.CompilerParams(vmem_limit_bytes=16 << 20),
    )(current, own, own_squares, *arrived)


def first_gram_body(table, kept, swapped, columns, result, turned, rows, arrived):
    @pl.when(table[20] == 1)
    def _():
        pltpu.make_async_copy(kept, rows, arrived).start()

    @pl.when(table[20] == 0)
    def _():
        pltpu.make_async_copy(swapped, rows, arrived).start()

    pltpu.make_async_copy(rows, rows, arrived).wait()
    right = columns[...]
    for b in range(NBLK):
        left = rows[b].T
        turned[b * LANE : (b + 1) * LANE, :] = left
        result[b] = jnp.dot(left, right, preferred_element_type=jnp.float32) * (1.0 / TOKENS)


def first_gram(table, kept, swapped, columns):
    return pl.pallas_call(
        first_gram_body,
        out_shape=[
            jax.ShapeDtypeStruct((NBLK, LANE, LANE), jnp.float32),
            jax.ShapeDtypeStruct((NBLK * LANE, TOKENS), jnp.bfloat16),
        ],
        in_specs=[IN_SMEM, IN_PLACE, IN_PLACE, IN_VMEM],
        out_specs=[IN_VMEM] * 2,
        scratch_shapes=[pltpu.VMEM((NBLK, TOKENS, LANE), jnp.bfloat16), pltpu.SemaphoreType.DMA],
        name="first_gram",
        cost_estimate=pl.CostEstimate(flops=2 * TOKENS * 2048 * LANE, bytes_accessed=5 << 20, transcendentals=0),
        compiler_params=pltpu.CompilerParams(vmem_limit_bytes=24 << 20),
    )(table, kept, swapped, columns)


def gram_body(turned, columns, result):
    total = jnp.dot(turned[...], columns[...], preferred_element_type=jnp.float32)
    result[...] = total.reshape(NBLK, LANE, LANE) * (1.0 / TOKENS)


def gram(turned, columns):
    return pl.pallas_call(
        gram_body,
        out_shape=jax.ShapeDtypeStruct((NBLK, LANE, LANE), jnp.float32),
        in_specs=[IN_VMEM] * 2,
        out_specs=IN_VMEM,
        name="gram",
        cost_estimate=pl.CostEstimate(flops=2 * TOKENS * 2048 * LANE, bytes_accessed=3 << 20, transcendentals=0),
        compiler_params=pltpu.CompilerParams(vmem_limit_bytes=16 << 20),
    )(turned, columns)


def quarter_of_section(block):
    own_quarter = 2 * lax.axis_index("xl") + lax.axis_index("c") == lax.axis_index("y")
    across = send(
        block, ("y", "xl", "c"), (NY, 2, 2), lambda y, xl, c: (y, 1 - xl, c) if 2 * xl + c == y else None
    )
    here = jnp.where(own_quarter, block, across)
    beside = send(here, ("y", "xl", "c"), (NY, 2, 2), lambda y, xl, c: (y, xl, 1 - c) if c == y % 2 else None)
    return jnp.where(lax.axis_index("c") == lax.axis_index("y") % 2, here, beside)


def local(block_in, weights, gains, layer_counts):
    section = lax.axis_index("y")
    sections = jnp.arange(NY, dtype=jnp.int32)
    start = jnp.sum(jnp.where(sections < section, layer_counts, 0))
    layers = jnp.arange(LAYERS, dtype=jnp.int32)
    slots = jnp.clip(layers - start, 0, SLOTS - 1)
    ends = jnp.sum(jnp.where(sections[None, :] <= sections[:3, None], layer_counts[None, :], 0), axis=1)
    hops = jnp.any(ends[:, None] == layers[None, :] + 1, axis=0)
    table = lax.dynamic_index_in_dim(
        jnp.asarray(block_table()), lax.axis_index(("z", "xh", "xl", "c")), 0, keepdims=False
    )

    stays = lax.axis_index("xh") == lax.axis_index("c")
    by_block = block_in.transpose(1, 0, 2).reshape(TOKENS, LANE)
    mine = jnp.where(stays, by_block, swap_roles(by_block))
    gains = gains.reshape(SLOTS * NBLK, 1, LANE)
    gains = jnp.where(stays, gains, swap_roles(gains))

    def tile(slot, after):
        held, _ = lax.optimization_barrier((weights, after))
        return jnp.where(stays, held[slot], swap_roles(held[slot]))

    early = first_round(mine)
    tiles = [tile(0, early[1])]
    whole = assemble(table, early + second_round(early))
    current = lax.dynamic_index_in_dim(
        whole, 2 * lax.axis_index("z") + lax.axis_index("c"), 0, keepdims=False
    )
    for layer in range(LAYERS):
        if layer:
            early = first_round(current)
            begun = begin(layer, table, slots, early, gains, tiles)
            late = second_round(early, begun[1])
        else:
            early = late = [whole]
            begun = begin(layer, table, slots, early, gains, tiles)
        outs = finish(layer, table, slots, late, gains, begun)
        arrived = [along_x(outs[k], k + 1) for k in range(3)]
        current = update(current, outs[3], outs[4], arrived)
        if layer < SLOTS - 1:
            tiles.append(tile(layer + 1, current))
        if layer == SLOTS:
            kept, _ = lax.optimization_barrier((whole, current))
            swapped = swap_roles(kept)
        if layer < LAYERS - 1:
            current = lax.cond(
                hops[layer],
                lambda v: send(v, ("y",), (NY,), lambda y: (y + 1,) if y < NY - 1 else None),
                lambda v: v,
                current,
            )

    at = 2 * lax.axis_index("z") + lax.axis_index("xh")
    x0 = jnp.where(
        stays,
        lax.dynamic_index_in_dim(whole, at, 0, keepdims=False),
        lax.dynamic_index_in_dim(swapped, at, 0, keepdims=False),
    )
    gram_in, turned = first_gram(table, whole, swapped, quarter_of_section(x0))

    copies = [
        send(
            current,
            ("xh", "y", "xl", "c"),
            (2, NY, 2, 2),
            lambda xh, y, xl, c, plane=plane: (c, plane, xl, xh) if y == NY - 1 else None,
        )
        for plane in range(NY)
    ]
    final = copies[0]
    for plane in range(1, NY):
        final = jnp.where(section == plane, copies[plane], final)
    block_out = lax.all_to_all(final.reshape(NBLK, TOKENS // NBLK, LANE), ("z", "xh"), 0, 0, tiled=True)
    gram_cross = gram(turned, quarter_of_section(final))
    shape = (NBLK, LANE, 1, LANE)
    return block_out.transpose(1, 0, 2), gram_in.reshape(shape), gram_cross.reshape(shape)


def solution(mesh):
    finer = Mesh(mesh.devices.reshape(NZ, 2, NY, 2, 2), AXES)
    dp, section, tensor = ("z", "xh"), "y", ("xl", "c")
    return jax.shard_map(
        local,
        mesh=finer,
        in_specs=(P(dp, None, tensor), P(section, None, tensor, dp), P(section, None, tensor), P()),
        out_specs=(P(dp, None, tensor), P(None, tensor, dp, section), P(None, tensor, dp, section)),
        check_vma=False,
    )
```

```python
import functools
import jax
import jax.numpy as jnp
import numpy as np
from jax import lax
from jax.experimental import pallas as pl
from jax.experimental.pallas import tpu as pltpu
from jax.sharding import Mesh, PartitionSpec as P

D = 8192
SLOTS = 3
LAYERS = 8
TOKENS = 512
NBLK = 16
LANE = 128
NZ = 8
NY = 4
EPSILON = 1e-05
TAIL = 16
GROUPS = TOKENS // LANE
EARLY = 10
LATE = NBLK - EARLY
AXES = ("z", "xh", "y", "xl", "c")
IN_VMEM = pl.BlockSpec(memory_space=pltpu.VMEM)
IN_SMEM = pl.BlockSpec(memory_space=pltpu.SMEM)
IN_PLACE = pl.BlockSpec(memory_space=pltpu.HBM)


def send(array, axes, sizes, route):
    pairs = []
    for source in np.ndindex(*sizes):
        target = route(*source)
        if target is not None:
            pairs.append((int(np.ravel_multi_index(source, sizes)), int(np.ravel_multi_index(target, sizes))))
    return lax.ppermute(array, axes, pairs)


def swap_roles(array):
    return send(array, ("xh", "c"), (2, 2), lambda xh, c: (c, xh) if xh != c else None)


def other_core(array):
    return send(array, ("c",), (2,), lambda c: (1 - c,))


def along_z(array, distance):
    return send(array, ("z", "c"), (NZ, 2), lambda z, c: ((z + distance * (1 - 2 * c)) % NZ, c))


def along_x(array, step):
    def route(xh, xl):
        place = (2 * xh + xl + step) % 4
        return place // 2, place % 2

    return send(array, ("xh", "xl"), (2, 2), route)


def first_round(block, other):
    chip = jnp.concatenate([block, other], axis=0)
    near, far = along_z(chip, 1), along_z(chip, 2)
    return [block, other, near, far]


def shared(parts, before=None):
    block, other, near, far = parts
    if before is not None:
        passed, _ = lax.optimization_barrier((far, before))
    else:
        passed = far
    return [block, other, near, other_core(near), far, other_core(passed)]


def finished_first(value, before):
    return lax.optimization_barrier((value, before))[0]


def second_round(parts, before=None):
    block, far = parts[0], parts[4]
    third, fourth = along_z(far, 1), along_z(far[: block.shape[0]], 2)
    if before is not None:
        third, fourth, _ = lax.optimization_barrier((third, fourth, before))
    return [third, other_core(third), fourth, other_core(fourth)]


def block_table():
    table = np.zeros((NZ, 2, 2, 2, 24), np.int32)
    for z, xh, xl, c in np.ndindex(NZ, 2, 2, 2):
        away = -1 if c == 0 else 1
        order = [(z, c), (z, 1 - c)]
        for r in range(1, 4):
            order += [(z + away * r, c), (z + away * r, 1 - c)]
            order += [(z - away * r, 1 - c), (z - away * r, c)]
        order += [(z + 4, c), (z + 4, 1 - c)]
        row = [2 * (at % NZ) + core for at, core in order]
        for step in range(4):
            place = (2 * xh + xl + step) % 4
            row.append(2 * (place % 2) + place // 2)
        row.append(int(xh == c))
        table[z, xh, xl, c, : len(row)] = row
    return table.reshape(-1, 24)


def pieces_of(refs):
    rows = min(ref.shape[0] for ref in refs)
    pieces = []
    for ref in refs:
        pieces += [ref[k * rows : (k + 1) * rows, :] for k in range(ref.shape[0] // rows)]
    return pieces


def assemble_body(table, *refs):
    parts, whole = refs[:-1], refs[-1]
    rows = TOKENS // NBLK
    for k, piece in enumerate(pieces_of(parts)):
        at = pl.multiple_of(table[k] * rows, rows)
        for b in range(NBLK):
            whole[b, pl.ds(at, rows), :] = piece[b * rows : (b + 1) * rows, :]


def assemble(table, parts):
    return pl.pallas_call(
        assemble_body,
        out_shape=jax.ShapeDtypeStruct((NBLK, TOKENS, LANE), jnp.bfloat16),
        in_specs=[IN_SMEM] + [IN_VMEM] * len(parts),
        out_specs=IN_VMEM,
        name="assemble",
        cost_estimate=pl.CostEstimate(flops=0, bytes_accessed=4 << 20, transcendentals=0),
        compiler_params=pltpu.CompilerParams(vmem_limit_bytes=24 << 20),
    )(table, *parts)


def in_three(value):
    first = value.astype(jnp.bfloat16)
    rest = value - first.astype(jnp.float32)
    second = rest.astype(jnp.bfloat16)
    third = (rest - second.astype(jnp.float32)).astype(jnp.bfloat16)
    return [first, second, third]


def scale_rows(pieces, gains, at, rows):
    squares = jnp.zeros((TOKENS, LANE), jnp.float32)
    for k, piece in enumerate(pieces):
        wide = piece.astype(jnp.float32)
        squares = squares + wide * wide
        rows[:, k * LANE : (k + 1) * LANE] = (wide * gains[at[k]]).astype(jnp.bfloat16)
    return squares


def fetch_body(layer, natural, table, slots, *refs):
    tiles, matrix, arrived = refs[:-2], refs[-2], refs[-1]
    slot, stays = slots[layer], table[20] == 1
    count = len(tiles) // 2
    for k in range(count):
        mine = slot >= k if k == count - 1 else slot == k
        for moved in range(2):

            @pl.when(jnp.logical_and(mine, jnp.logical_not(stays) if moved else stays))
            def _(tile=tiles[2 * k + moved]):
                for j in range(NBLK):
                    pltpu.make_async_copy(
                        tile.at[j if natural else table[j]], matrix.at[pl.ds(j * LANE, LANE), :], arrived
                    ).start()

    pltpu.make_async_copy(matrix, matrix, arrived).wait()


def fetch(layer, table, slots, tiles):
    flat = [tile for pair in tiles for tile in pair]
    return pl.pallas_call(
        functools.partial(fetch_body, layer, layer == 0),
        out_shape=jax.ShapeDtypeStruct((NBLK * LANE, 512), jnp.bfloat16),
        in_specs=[IN_SMEM] * 2 + [IN_PLACE] * len(flat),
        out_specs=IN_VMEM,
        scratch_shapes=[pltpu.SemaphoreType.DMA],
        name="fetch",
        cost_estimate=pl.CostEstimate(flops=0, bytes_accessed=8 << 20, transcendentals=0),
        compiler_params=pltpu.CompilerParams(vmem_limit_bytes=8 << 20),
    )(table, slots, *flat)


def begin_body(layer, n_parts, table, slots, *refs):
    parts, (gains, matrix, partial, squares, rows) = refs[:n_parts], refs[n_parts:]
    slot = slots[layer]
    order = list(range(NBLK)) if n_parts == 1 else [table[k] for k in range(NBLK)]
    pieces = [parts[0][b] for b in range(EARLY)] if n_parts == 1 else pieces_of(parts)
    squares[...] = scale_rows(pieces, gains, [slot * NBLK + b for b in order[:EARLY]], rows)
    for pair in range(2):
        total = jnp.dot(
            rows[...], matrix[: EARLY * LANE, pair * 256 : (pair + 1) * 256], preferred_element_type=jnp.float32
        )
        partial[2 * pair] = total[:, :LANE]
        partial[2 * pair + 1] = total[:, LANE:]


def begin(layer, table, slots, parts, gains, matrix):
    return pl.pallas_call(
        functools.partial(begin_body, layer, len(parts)),
        out_shape=[
            jax.ShapeDtypeStruct((4, TOKENS, LANE), jnp.float32),
            jax.ShapeDtypeStruct((TOKENS, LANE), jnp.float32),
        ],
        in_specs=[IN_SMEM] * 2 + [IN_VMEM] * (len(parts) + 2),
        out_specs=[IN_VMEM] * 2,
        scratch_shapes=[pltpu.VMEM((TOKENS, EARLY * LANE), jnp.bfloat16)],
        name="begin",
        cost_estimate=pl.CostEstimate(flops=2 * TOKENS * 1280 * 512, bytes_accessed=5 << 20, transcendentals=0),
        compiler_params=pltpu.CompilerParams(vmem_limit_bytes=16 << 20),
    )(table, slots, *parts, gains, matrix)


def finish_body(layer, n_parts, *refs):
    table, slots = refs[:2]
    parts = refs[2 : 2 + n_parts]
    gains, partial, squares, matrix = refs[2 + n_parts : 6 + n_parts]
    sends, own, own_squares, rows, product = refs[6 + n_parts : 9 + n_parts], *refs[9 + n_parts :]
    slot = slots[layer]
    if n_parts == 1:
        pieces, order = [parts[0][b] for b in range(EARLY, NBLK)], range(EARLY, NBLK)
    else:
        pieces, order = pieces_of(parts), [table[k] for k in range(EARLY, NBLK)]
    total = squares[...] + scale_rows(pieces, gains, [slot * NBLK + b for b in order], rows)
    for pair in range(2):
        both = jnp.dot(
            rows[...], matrix[EARLY * LANE :, pair * 256 : (pair + 1) * 256], preferred_element_type=jnp.float32
        )
        product[2 * pair] = both[:, :LANE]
        product[2 * pair + 1] = both[:, LANE:]
    sums = jnp.concatenate(
        [jnp.sum(total[a * LANE : (a + 1) * LANE].T, axis=0, keepdims=True) for a in range(GROUPS)], axis=0
    )
    own_squares[...] = sums
    tail = jnp.concatenate(in_three(sums) + [jnp.zeros((TAIL - 3 * GROUPS, LANE), jnp.bfloat16)], axis=0)
    own[...] = product[table[16]] + partial[table[16]]
    for step in range(1, 4):
        quarter = table[16 + step]
        sends[step - 1][0:TOKENS, :] = (product[quarter] + partial[quarter]).astype(jnp.bfloat16)
        sends[step - 1][TOKENS : TOKENS + TAIL, :] = tail


def finish(layer, table, slots, parts, gains, begun):
    outs = [jax.ShapeDtypeStruct((TOKENS + TAIL, LANE), jnp.bfloat16)] * 3
    outs += [jax.ShapeDtypeStruct((TOKENS, LANE), jnp.float32), jax.ShapeDtypeStruct((GROUPS, LANE), jnp.float32)]
    return pl.pallas_call(
        functools.partial(finish_body, layer, len(parts)),
        out_shape=outs,
        in_specs=[IN_SMEM] * 2 + [IN_VMEM] * (len(parts) + 4),
        out_specs=[IN_VMEM] * 5,
        scratch_shapes=[
            pltpu.VMEM((TOKENS, LATE * LANE), jnp.bfloat16),
            pltpu.VMEM((4, TOKENS, LANE), jnp.float32),
        ],
        name="finish",
        cost_estimate=pl.CostEstimate(flops=2 * TOKENS * 768 * 512, bytes_accessed=5 << 20, transcendentals=0),
        compiler_params=pltpu.CompilerParams(vmem_limit_bytes=24 << 20),
    )(table, slots, *parts, gains, *begun)


def update_body(current, own, own_squares, *refs):
    arrived, result = refs[:3], refs[3]
    total, squares = own[...], own_squares[...]
    for ref in arrived:
        total = total + ref[0:TOKENS, :].astype(jnp.float32)
        tail = ref[TOKENS : TOKENS + TAIL, :].astype(jnp.float32)
        squares = squares + (tail[0:GROUPS] + tail[GROUPS : 2 * GROUPS] + tail[2 * GROUPS : 3 * GROUPS])
    scale = lax.rsqrt(squares * (1.0 / D) + EPSILON)
    column = jnp.concatenate(
        [jnp.broadcast_to(scale[a : a + 1], (LANE, LANE)).T for a in range(GROUPS)], axis=0
    )
    step = (total * column).astype(jnp.bfloat16).astype(jnp.float32)
    result[...] = (current[...].astype(jnp.float32) + step).astype(jnp.bfloat16)


def update(current, own, own_squares, arrived):
    return pl.pallas_call(
        update_body,
        out_shape=jax.ShapeDtypeStruct((TOKENS, LANE), jnp.bfloat16),
        in_specs=[IN_VMEM] * 6,
        out_specs=IN_VMEM,
        name="update",
        cost_estimate=pl.CostEstimate(flops=20 * TOKENS * LANE, bytes_accessed=1 << 20, transcendentals=512),
        compiler_params=pltpu.CompilerParams(vmem_limit_bytes=16 << 20),
    )(current, own, own_squares, *arrived)


def first_gram_body(table, kept, swapped, columns, result, turned, rows, arrived):
    @pl.when(table[20] == 1)
    def _():
        pltpu.make_async_copy(kept, rows, arrived).start()

    @pl.when(table[20] == 0)
    def _():
        pltpu.make_async_copy(swapped, rows, arrived).start()

    pltpu.make_async_copy(rows, rows, arrived).wait()
    right = columns[...]
    for b in range(NBLK):
        left = rows[b].T
        turned[b * LANE : (b + 1) * LANE, :] = left
        result[b] = jnp.dot(left, right, preferred_element_type=jnp.float32) * (1.0 / TOKENS)


def first_gram(table, kept, swapped, columns):
    return pl.pallas_call(
        first_gram_body,
        out_shape=[
            jax.ShapeDtypeStruct((NBLK, LANE, LANE), jnp.float32),
            jax.ShapeDtypeStruct((NBLK * LANE, TOKENS), jnp.bfloat16),
        ],
        in_specs=[IN_SMEM, IN_PLACE, IN_PLACE, IN_VMEM],
        out_specs=[IN_VMEM] * 2,
        scratch_shapes=[pltpu.VMEM((NBLK, TOKENS, LANE), jnp.bfloat16), pltpu.SemaphoreType.DMA],
        name="first_gram",
        cost_estimate=pl.CostEstimate(flops=2 * TOKENS * 2048 * LANE, bytes_accessed=5 << 20, transcendentals=0),
        compiler_params=pltpu.CompilerParams(vmem_limit_bytes=24 << 20),
    )(table, kept, swapped, columns)


def gram_body(turned, columns, result):
    total = jnp.dot(turned[...], columns[...], preferred_element_type=jnp.float32)
    result[...] = total.reshape(NBLK, LANE, LANE) * (1.0 / TOKENS)


def gram(turned, columns):
    return pl.pallas_call(
        gram_body,
        out_shape=jax.ShapeDtypeStruct((NBLK, LANE, LANE), jnp.float32),
        in_specs=[IN_VMEM] * 2,
        out_specs=IN_VMEM,
        name="gram",
        cost_estimate=pl.CostEstimate(flops=2 * TOKENS * 2048 * LANE, bytes_accessed=3 << 20, transcendentals=0),
        compiler_params=pltpu.CompilerParams(vmem_limit_bytes=16 << 20),
    )(turned, columns)


def quarter_of_section(block):
    own_quarter = 2 * lax.axis_index("xl") + lax.axis_index("c") == lax.axis_index("y")
    across = send(
        block, ("y", "xl", "c"), (NY, 2, 2), lambda y, xl, c: (y, 1 - xl, c) if 2 * xl + c == y else None
    )
    here = jnp.where(own_quarter, block, across)
    beside = send(here, ("y", "xl", "c"), (NY, 2, 2), lambda y, xl, c: (y, xl, 1 - c) if c == y % 2 else None)
    return jnp.where(lax.axis_index("c") == lax.axis_index("y") % 2, here, beside)


def local(block_in, weights, gains, layer_counts):
    section = lax.axis_index("y")
    sections = jnp.arange(NY, dtype=jnp.int32)
    start = jnp.sum(jnp.where(sections < section, layer_counts, 0))
    layers = jnp.arange(LAYERS, dtype=jnp.int32)
    slots = jnp.clip(layers - start, 0, SLOTS - 1)
    ends = jnp.sum(jnp.where(sections[None, :] <= sections[:3, None], layer_counts[None, :], 0), axis=1)
    hops = jnp.any(ends[:, None] == layers[None, :] + 1, axis=0)
    table = lax.dynamic_index_in_dim(
        jnp.asarray(block_table()), lax.axis_index(("z", "xh", "xl", "c")), 0, keepdims=False
    )

    stays = lax.axis_index("xh") == lax.axis_index("c")
    by_block = block_in.transpose(1, 0, 2).reshape(TOKENS, LANE)
    mine = jnp.where(stays, by_block, swap_roles(by_block))
    gains = gains.reshape(SLOTS * NBLK, 1, LANE)
    gains = jnp.where(stays, gains, swap_roles(gains))

    def tile(slot, early, after):
        kept = finished_first(weights, early)[slot]
        return kept, swap_roles(finished_first(kept, after))

    other = other_core(mine)
    early = shared(first_round(mine, other))
    tiles = [tile(0, mine, other)]
    whole = assemble(table, early + second_round(early))
    current = lax.dynamic_index_in_dim(
        whole, 2 * lax.axis_index("z") + lax.axis_index("c"), 0, keepdims=False
    )
    turned = None
    for layer in range(LAYERS):
        if layer:
            other = other_core(current)
            matrix = fetch(layer, table, finished_first(slots, other), tiles)
            early = shared(first_round(current, other), matrix)
            begun = begin(
                layer, table, slots if turned is None else finished_first(slots, turned), early, gains, matrix
            )
            late = second_round(early, begun[1])
        else:
            matrix = fetch(layer, table, slots, tiles)
            early = late = [whole]
            begun = begin(layer, table, slots, early, gains, matrix)
        outs = finish(layer, table, slots, late, gains, [*begun, matrix])
        arrived = [along_x(outs[k], k + 1) for k in range(3)]
        current = update(current, outs[3], outs[4], arrived)
        if layer < SLOTS - 1:
            tiles.append(tile(layer + 1, outs[4], current))
        if layer == SLOTS:
            swapped = swap_roles(finished_first(whole, current))
        if layer == LAYERS - 2:
            at = 2 * lax.axis_index("z") + lax.axis_index("xh")
            x0 = jnp.where(
                stays,
                lax.dynamic_index_in_dim(whole, at, 0, keepdims=False),
                lax.dynamic_index_in_dim(swapped, at, 0, keepdims=False),
            )
            gram_in, turned = first_gram(table, whole, swapped, quarter_of_section(x0))
        if layer < LAYERS - 1:
            current = lax.cond(
                hops[layer],
                lambda v: send(v, ("y",), (NY,), lambda y: (y + 1,) if y < NY - 1 else None),
                lambda v: v,
                current,
            )

    copies = [
        send(
            current,
            ("xh", "y", "xl", "c"),
            (2, NY, 2, 2),
            lambda xh, y, xl, c, plane=plane: (c, plane, xl, xh) if y == NY - 1 else None,
        )
        for plane in range(NY)
    ]
    final = copies[0]
    for plane in range(1, NY):
        final = jnp.where(section == plane, copies[plane], final)
    block_out = lax.all_to_all(final.reshape(NBLK, TOKENS // NBLK, LANE), ("z", "xh"), 0, 0, tiled=True)
    gram_cross = gram(turned, quarter_of_section(final))
    block_out = finished_first(block_out, gram_cross)
    shape = (NBLK, LANE, 1, LANE)
    return block_out.transpose(1, 0, 2), gram_in.reshape(shape), gram_cross.reshape(shape)


def solution(mesh):
    finer = Mesh(mesh.devices.reshape(NZ, 2, NY, 2, 2), AXES)
    dp, section, tensor = ("z", "xh"), "y", ("xl", "c")
    return jax.shard_map(
        local,
        mesh=finer,
        in_specs=(P(dp, None, tensor), P(section, None, tensor, dp), P(section, None, tensor), P()),
        out_specs=(P(dp, None, tensor), P(None, tensor, dp, section), P(None, tensor, dp, section)),
        check_vma=False,
    )
```

```python
import functools
import jax
import jax.numpy as jnp
import numpy as np
from jax import lax
from jax.experimental import pallas as pl
from jax.experimental.pallas import tpu as pltpu
from jax.sharding import Mesh, PartitionSpec as P

D = 8192
SLOTS = 3
LAYERS = 8
TOKENS = 512
NBLK = 16
LANE = 128
NZ = 8
NY = 4
EPSILON = 1e-05
TAIL = 16
GROUPS = TOKENS // LANE
EARLY = 10
LATE = NBLK - EARLY
AXES = ("z", "xh", "y", "xl", "c")
IN_VMEM = pl.BlockSpec(memory_space=pltpu.VMEM)
IN_SMEM = pl.BlockSpec(memory_space=pltpu.SMEM)
IN_PLACE = pl.BlockSpec(memory_space=pltpu.HBM)


def send(array, axes, sizes, route):
    pairs = []
    for source in np.ndindex(*sizes):
        target = route(*source)
        if target is not None:
            pairs.append((int(np.ravel_multi_index(source, sizes)), int(np.ravel_multi_index(target, sizes))))
    return lax.ppermute(array, axes, pairs)


def swap_roles(array):
    return send(array, ("xh", "c"), (2, 2), lambda xh, c: (c, xh) if xh != c else None)


def other_core(array):
    return send(array, ("c",), (2,), lambda c: (1 - c,))


def along_z(array, distance):
    return send(array, ("z", "c"), (NZ, 2), lambda z, c: ((z + distance * (1 - 2 * c)) % NZ, c))


def along_x(array, step):
    def route(xh, xl):
        place = (2 * xh + xl + step) % 4
        return place // 2, place % 2

    return send(array, ("xh", "xl"), (2, 2), route)


def first_round(block, other):
    chip = jnp.concatenate([block, other], axis=0)
    near, far = along_z(chip, 1), along_z(chip, 2)
    return [block, other, near, far]


def shared(parts, before=None):
    block, other, near, far = parts
    if before is not None:
        passed, _ = lax.optimization_barrier((far, before))
    else:
        passed = far
    return [block, other, near, other_core(near), far, other_core(passed)]


def finished_first(value, before):
    return lax.optimization_barrier((value, before))[0]


def second_round(parts, before=None):
    block, far = parts[0], parts[4]
    third, fourth = along_z(far, 1), along_z(far[: block.shape[0]], 2)
    if before is not None:
        third, fourth, _ = lax.optimization_barrier((third, fourth, before))
    return [third, other_core(third), fourth, other_core(fourth)]


def block_table():
    table = np.zeros((NZ, 2, 2, 2, 40), np.int32)
    for z, xh, xl, c in np.ndindex(NZ, 2, 2, 2):
        away = -1 if c == 0 else 1
        order = [(z, c), (z, 1 - c)]
        for r in range(1, 4):
            order += [(z + away * r, c), (z + away * r, 1 - c)]
            order += [(z - away * r, 1 - c), (z - away * r, c)]
        order += [(z + 4, c), (z + 4, 1 - c)]
        row = [2 * (at % NZ) + core for at, core in order]
        for step in range(4):
            place = (2 * xh + xl + step) % 4
            row.append(2 * (place % 2) + place // 2)
        row.append(int(xh == c))
        table[z, xh, xl, c, : len(row)] = row
        table[z, xh, xl, c, 24:] = np.argsort(row[:NBLK])
    return table.reshape(-1, 40)


def pieces_of(refs):
    rows = min(ref.shape[0] for ref in refs)
    pieces = []
    for ref in refs:
        pieces += [ref[k * rows : (k + 1) * rows, :] for k in range(ref.shape[0] // rows)]
    return pieces


def assemble_body(table, *refs):
    parts, whole = refs[:-1], refs[-1]
    rows = TOKENS // NBLK
    for k, piece in enumerate(pieces_of(parts)):
        at = pl.multiple_of(table[k] * rows, rows)
        for b in range(NBLK):
            whole[b, pl.ds(at, rows), :] = piece[b * rows : (b + 1) * rows, :]


def assemble(table, parts):
    return pl.pallas_call(
        assemble_body,
        out_shape=jax.ShapeDtypeStruct((NBLK, TOKENS, LANE), jnp.bfloat16),
        in_specs=[IN_SMEM] + [IN_VMEM] * len(parts),
        out_specs=IN_VMEM,
        name="assemble",
        cost_estimate=pl.CostEstimate(flops=0, bytes_accessed=4 << 20, transcendentals=0),
        compiler_params=pltpu.CompilerParams(vmem_limit_bytes=24 << 20),
    )(table, *parts)


def in_three(value):
    first = value.astype(jnp.bfloat16)
    rest = value - first.astype(jnp.float32)
    second = rest.astype(jnp.bfloat16)
    third = (rest - second.astype(jnp.float32)).astype(jnp.bfloat16)
    return [first, second, third]


def scale_rows(pieces, gains, at, rows):
    squares = jnp.zeros((TOKENS, LANE), jnp.float32)
    for k, piece in enumerate(pieces):
        wide = piece.astype(jnp.float32)
        squares = squares + wide * wide
        rows[:, k * LANE : (k + 1) * LANE] = (wide * gains[at[k]]).astype(jnp.bfloat16)
    return squares


def fetch_body(layer, natural, counts, table, slots, *refs):
    pieces, matrix, arrived = list(refs[:-2]), refs[-2], refs[-1]
    slot, stays = slots[layer], table[20] == 1
    for k, count in enumerate(counts):
        mine = slot >= k if k == len(counts) - 1 else slot == k
        for moved in range(2):
            chosen = [pieces.pop(0) for _ in range(count)]

            @pl.when(jnp.logical_and(mine, jnp.logical_not(stays) if moved else stays))
            def _(chosen=chosen):
                per = NBLK // len(chosen)
                for b in range(NBLK):
                    at = b if natural else table[24 + b]
                    pltpu.make_async_copy(
                        chosen[b // per].at[b % per], matrix.at[pl.ds(pl.multiple_of(at * LANE, LANE), LANE), :], arrived
                    ).start()

    pltpu.make_async_copy(matrix, matrix, arrived).wait()


def fetch(layer, table, slots, tiles):
    flat, counts = [], []
    for pieces in tiles:
        flat += [own for own, _ in pieces] + [moved for _, moved in pieces]
        counts.append(len(pieces))
    return pl.pallas_call(
        functools.partial(fetch_body, layer, layer == 0, counts),
        out_shape=jax.ShapeDtypeStruct((NBLK * LANE, 512), jnp.bfloat16),
        in_specs=[IN_SMEM] * 2 + [IN_PLACE] * len(flat),
        out_specs=IN_VMEM,
        scratch_shapes=[pltpu.SemaphoreType.DMA],
        name="fetch",
        cost_estimate=pl.CostEstimate(flops=0, bytes_accessed=8 << 20, transcendentals=0),
        compiler_params=pltpu.CompilerParams(vmem_limit_bytes=8 << 20),
    )(table, slots, *flat)


def begin_body(layer, n_parts, table, slots, *refs):
    parts, (gains, matrix, partial, squares, rows) = refs[:n_parts], refs[n_parts:]
    slot = slots[layer]
    order = list(range(NBLK)) if n_parts == 1 else [table[k] for k in range(NBLK)]
    pieces = [parts[0][b] for b in range(EARLY)] if n_parts == 1 else pieces_of(parts)
    squares[...] = scale_rows(pieces, gains, [slot * NBLK + b for b in order[:EARLY]], rows)
    for pair in range(2):
        total = jnp.dot(
            rows[...], matrix[: EARLY * LANE, pair * 256 : (pair + 1) * 256], preferred_element_type=jnp.float32
        )
        partial[2 * pair] = total[:, :LANE]
        partial[2 * pair + 1] = total[:, LANE:]


def begin(layer, table, slots, parts, gains, matrix):
    return pl.pallas_call(
        functools.partial(begin_body, layer, len(parts)),
        out_shape=[
            jax.ShapeDtypeStruct((4, TOKENS, LANE), jnp.float32),
            jax.ShapeDtypeStruct((TOKENS, LANE), jnp.float32),
        ],
        in_specs=[IN_SMEM] * 2 + [IN_VMEM] * (len(parts) + 2),
        out_specs=[IN_VMEM] * 2,
        scratch_shapes=[pltpu.VMEM((TOKENS, EARLY * LANE), jnp.bfloat16)],
        name="begin",
        cost_estimate=pl.CostEstimate(flops=2 * TOKENS * 1280 * 512, bytes_accessed=5 << 20, transcendentals=0),
        compiler_params=pltpu.CompilerParams(vmem_limit_bytes=16 << 20),
    )(table, slots, *parts, gains, matrix)


def finish_body(layer, n_parts, *refs):
    table, slots = refs[:2]
    parts = refs[2 : 2 + n_parts]
    gains, partial, squares, matrix = refs[2 + n_parts : 6 + n_parts]
    sends, own, own_squares, rows, product = refs[6 + n_parts : 9 + n_parts], *refs[9 + n_parts :]
    slot = slots[layer]
    if n_parts == 1:
        pieces, order = [parts[0][b] for b in range(EARLY, NBLK)], range(EARLY, NBLK)
    else:
        pieces, order = pieces_of(parts), [table[k] for k in range(EARLY, NBLK)]
    total = squares[...] + scale_rows(pieces, gains, [slot * NBLK + b for b in order], rows)
    for pair in range(2):
        both = jnp.dot(
            rows[...], matrix[EARLY * LANE :, pair * 256 : (pair + 1) * 256], preferred_element_type=jnp.float32
        )
        product[2 * pair] = both[:, :LANE]
        product[2 * pair + 1] = both[:, LANE:]
    sums = jnp.concatenate(
        [jnp.sum(total[a * LANE : (a + 1) * LANE].T, axis=0, keepdims=True) for a in range(GROUPS)], axis=0
    )
    own_squares[...] = sums
    tail = jnp.concatenate(in_three(sums) + [jnp.zeros((TAIL - 3 * GROUPS, LANE), jnp.bfloat16)], axis=0)
    own[...] = product[table[16]] + partial[table[16]]
    for step in range(1, 4):
        quarter = table[16 + step]
        sends[step - 1][0:TOKENS, :] = (product[quarter] + partial[quarter]).astype(jnp.bfloat16)
        sends[step - 1][TOKENS : TOKENS + TAIL, :] = tail


def finish(layer, table, slots, parts, gains, begun):
    outs = [jax.ShapeDtypeStruct((TOKENS + TAIL, LANE), jnp.bfloat16)] * 3
    outs += [jax.ShapeDtypeStruct((TOKENS, LANE), jnp.float32), jax.ShapeDtypeStruct((GROUPS, LANE), jnp.float32)]
    return pl.pallas_call(
        functools.partial(finish_body, layer, len(parts)),
        out_shape=outs,
        in_specs=[IN_SMEM] * 2 + [IN_VMEM] * (len(parts) + 4),
        out_specs=[IN_VMEM] * 5,
        scratch_shapes=[
            pltpu.VMEM((TOKENS, LATE * LANE), jnp.bfloat16),
            pltpu.VMEM((4, TOKENS, LANE), jnp.float32),
        ],
        name="finish",
        cost_estimate=pl.CostEstimate(flops=2 * TOKENS * 768 * 512, bytes_accessed=5 << 20, transcendentals=0),
        compiler_params=pltpu.CompilerParams(vmem_limit_bytes=24 << 20),
    )(table, slots, *parts, gains, *begun)


def update_body(current, own, own_squares, *refs):
    arrived, result = refs[:3], refs[3]
    total, squares = own[...], own_squares[...]
    for ref in arrived:
        total = total + ref[0:TOKENS, :].astype(jnp.float32)
        tail = ref[TOKENS : TOKENS + TAIL, :].astype(jnp.float32)
        squares = squares + (tail[0:GROUPS] + tail[GROUPS : 2 * GROUPS] + tail[2 * GROUPS : 3 * GROUPS])
    scale = lax.rsqrt(squares * (1.0 / D) + EPSILON)
    column = jnp.concatenate(
        [jnp.broadcast_to(scale[a : a + 1], (LANE, LANE)).T for a in range(GROUPS)], axis=0
    )
    step = (total * column).astype(jnp.bfloat16).astype(jnp.float32)
    result[...] = (current[...].astype(jnp.float32) + step).astype(jnp.bfloat16)


def update(current, own, own_squares, arrived):
    return pl.pallas_call(
        update_body,
        out_shape=jax.ShapeDtypeStruct((TOKENS, LANE), jnp.bfloat16),
        in_specs=[IN_VMEM] * 6,
        out_specs=IN_VMEM,
        name="update",
        cost_estimate=pl.CostEstimate(flops=20 * TOKENS * LANE, bytes_accessed=1 << 20, transcendentals=512),
        compiler_params=pltpu.CompilerParams(vmem_limit_bytes=16 << 20),
    )(current, own, own_squares, *arrived)


def first_gram_body(table, kept, swapped, columns, result, turned, rows, arrived):
    @pl.when(table[20] == 1)
    def _():
        pltpu.make_async_copy(kept, rows, arrived).start()

    @pl.when(table[20] == 0)
    def _():
        pltpu.make_async_copy(swapped, rows, arrived).start()

    pltpu.make_async_copy(rows, rows, arrived).wait()
    right = columns[...]
    for b in range(NBLK):
        left = rows[b].T
        turned[b * LANE : (b + 1) * LANE, :] = left
        result[b] = jnp.dot(left, right, preferred_element_type=jnp.float32) * (1.0 / TOKENS)


def first_gram(table, kept, swapped, columns):
    return pl.pallas_call(
        first_gram_body,
        out_shape=[
            jax.ShapeDtypeStruct((NBLK, LANE, LANE), jnp.float32),
            jax.ShapeDtypeStruct((NBLK * LANE, TOKENS), jnp.bfloat16),
        ],
        in_specs=[IN_SMEM, IN_PLACE, IN_PLACE, IN_VMEM],
        out_specs=[IN_VMEM] * 2,
        scratch_shapes=[pltpu.VMEM((NBLK, TOKENS, LANE), jnp.bfloat16), pltpu.SemaphoreType.DMA],
        name="first_gram",
        cost_estimate=pl.CostEstimate(flops=2 * TOKENS * 2048 * LANE, bytes_accessed=5 << 20, transcendentals=0),
        compiler_params=pltpu.CompilerParams(vmem_limit_bytes=24 << 20),
    )(table, kept, swapped, columns)


def gram_body(turned, columns, result):
    total = jnp.dot(turned[...], columns[...], preferred_element_type=jnp.float32)
    result[...] = total.reshape(NBLK, LANE, LANE) * (1.0 / TOKENS)


def gram(turned, columns):
    return pl.pallas_call(
        gram_body,
        out_shape=jax.ShapeDtypeStruct((NBLK, LANE, LANE), jnp.float32),
        in_specs=[IN_VMEM] * 2,
        out_specs=IN_VMEM,
        name="gram",
        cost_estimate=pl.CostEstimate(flops=2 * TOKENS * 2048 * LANE, bytes_accessed=3 << 20, transcendentals=0),
        compiler_params=pltpu.CompilerParams(vmem_limit_bytes=16 << 20),
    )(turned, columns)


def quarter_of_section(block, across=None):
    own_quarter = 2 * lax.axis_index("xl") + lax.axis_index("c") == lax.axis_index("y")
    if across is None:
        across = send(
            block, ("y", "xl", "c"), (NY, 2, 2), lambda y, xl, c: (y, 1 - xl, c) if 2 * xl + c == y else None
        )
    here = jnp.where(own_quarter, block, across)
    beside = send(here, ("y", "xl", "c"), (NY, 2, 2), lambda y, xl, c: (y, xl, 1 - c) if c == y % 2 else None)
    return jnp.where(lax.axis_index("c") == lax.axis_index("y") % 2, here, beside)


def local(block_in, weights, gains, layer_counts):
    section = lax.axis_index("y")
    sections = jnp.arange(NY, dtype=jnp.int32)
    start = jnp.sum(jnp.where(sections < section, layer_counts, 0))
    layers = jnp.arange(LAYERS, dtype=jnp.int32)
    slots = jnp.clip(layers - start, 0, SLOTS - 1)
    ends = jnp.sum(jnp.where(sections[None, :] <= sections[:3, None], layer_counts[None, :], 0), axis=1)
    hops = jnp.any(ends[:, None] == layers[None, :] + 1, axis=0)
    table = lax.dynamic_index_in_dim(
        jnp.asarray(block_table()), lax.axis_index(("z", "xh", "xl", "c")), 0, keepdims=False
    )

    stays = lax.axis_index("xh") == lax.axis_index("c")
    by_block = block_in.transpose(1, 0, 2).reshape(TOKENS, LANE)
    mine = jnp.where(stays, by_block, swap_roles(by_block))
    gains = gains.reshape(SLOTS * NBLK, 1, LANE)
    gains = jnp.where(stays, gains, swap_roles(gains))

    def piece(slot, first, count, early, after=None):
        kept = finished_first(weights, early)[slot, first : first + count]
        return kept, swap_roles(kept if after is None else finished_first(kept, after))

    other = other_core(mine)
    early = shared(first_round(mine, other))
    tiles = [[piece(0, 0, NBLK, mine, other)]]
    whole = assemble(table, early + second_round(early))
    current = lax.dynamic_index_in_dim(
        whole, 2 * lax.axis_index("z") + lax.axis_index("c"), 0, keepdims=False
    )
    turned = None
    for layer in range(LAYERS):
        if layer:
            other = other_core(current)
            matrix = fetch(layer, table, finished_first(slots, other), tiles)
            early = shared(first_round(current, other), matrix)
            begun = begin(
                layer, table, slots if turned is None else finished_first(slots, turned), early, gains, matrix
            )
            before = [begun[1]]
            if layer == 1:
                pieces = [piece(2, 4 * k, 4, matrix) for k in range(2)]
                before += [moved for _, moved in pieces]
                pieces.append(piece(2, 8, 4, begun[1]))
            late = second_round(early, before)
        else:
            matrix = fetch(layer, table, slots, tiles)
            early = late = [whole]
            begun = begin(layer, table, slots, early, gains, matrix)
            pieces = [piece(1, 4 * k, 4, whole) for k in range(2)]
        outs = finish(layer, table, slots, late, gains, [*begun, matrix])
        arrived = [along_x(outs[k], k + 1) for k in range(3)]
        if layer == 0:
            arrived = finished_first(arrived, [moved for _, moved in pieces])
        current = update(current, outs[3], outs[4], arrived)
        if layer == 0:
            tiles.append(pieces + [piece(1, 8, 4, outs[4]), piece(1, 12, 4, outs[4], current)])
        if layer == 1:
            tiles.append(pieces + [piece(2, 12, 4, outs[4])])
        if layer == SLOTS:
            swapped = swap_roles(finished_first(whole, current))
        if layer == LAYERS - 2:
            at = 2 * lax.axis_index("z") + lax.axis_index("xh")
            x0 = jnp.where(
                stays,
                lax.dynamic_index_in_dim(whole, at, 0, keepdims=False),
                lax.dynamic_index_in_dim(swapped, at, 0, keepdims=False),
            )
            gram_in, turned = first_gram(table, whole, swapped, quarter_of_section(x0))
        if layer < LAYERS - 1:
            current = lax.cond(
                hops[layer],
                lambda v: send(v, ("y",), (NY,), lambda y: (y + 1,) if y < NY - 1 else None),
                lambda v: v,
                current,
            )

    copies = [
        send(
            current,
            ("xh", "y", "xl", "c"),
            (2, NY, 2, 2),
            lambda xh, y, xl, c, plane=plane: (c, plane, xl, xh) if y == NY - 1 else None,
        )
        for plane in range(NY)
    ]
    across = send(
        current,
        ("xh", "y", "xl", "c"),
        (2, NY, 2, 2),
        lambda xh, y, xl, c: (c, 2 * xl + xh, 1 - xl, xh) if y == NY - 1 else None,
    )
    final = copies[0]
    for plane in range(1, NY):
        final = jnp.where(section == plane, copies[plane], final)
    block_out = lax.all_to_all(final.reshape(NBLK, TOKENS // NBLK, LANE), ("z", "xh"), 0, 0, tiled=True)
    gram_cross = gram(turned, quarter_of_section(final, across))
    block_out = finished_first(block_out, gram_cross)
    shape = (NBLK, LANE, 1, LANE)
    return block_out.transpose(1, 0, 2), gram_in.reshape(shape), gram_cross.reshape(shape)


def solution(mesh):
    finer = Mesh(mesh.devices.reshape(NZ, 2, NY, 2, 2), AXES)
    dp, section, tensor = ("z", "xh"), "y", ("xl", "c")
    return jax.shard_map(
        local,
        mesh=finer,
        in_specs=(P(dp, None, tensor), P(section, None, tensor, dp), P(section, None, tensor), P()),
        out_specs=(P(dp, None, tensor), P(None, tensor, dp, section), P(None, tensor, dp, section)),
        check_vma=False,
    )
```

```python
import functools
import jax
import jax.numpy as jnp
import numpy as np
from jax import lax
from jax.experimental import pallas as pl
from jax.experimental.pallas import tpu as pltpu
from jax.sharding import Mesh, PartitionSpec as P

D = 8192
SLOTS = 3
LAYERS = 8
TOKENS = 512
NBLK = 16
LANE = 128
NZ = 8
NY = 4
EPSILON = 1e-05
TAIL = 16
GROUPS = TOKENS // LANE
EARLY = 10
PIECES = 4
LATE = NBLK - EARLY
AXES = ("z", "xh", "y", "xl", "c")
IN_VMEM = pl.BlockSpec(memory_space=pltpu.VMEM)
IN_SMEM = pl.BlockSpec(memory_space=pltpu.SMEM)
IN_PLACE = pl.BlockSpec(memory_space=pltpu.HBM)


def send(array, axes, sizes, route):
    pairs = []
    for source in np.ndindex(*sizes):
        target = route(*source)
        if target is not None:
            pairs.append((int(np.ravel_multi_index(source, sizes)), int(np.ravel_multi_index(target, sizes))))
    return lax.ppermute(array, axes, pairs)


def swap_roles(array):
    return send(array, ("xh", "c"), (2, 2), lambda xh, c: (c, xh) if xh != c else None)


def other_core(array):
    return send(array, ("c",), (2,), lambda c: (1 - c,))


def along_z(array, distance):
    return send(array, ("z", "c"), (NZ, 2), lambda z, c: ((z + distance * (1 - 2 * c)) % NZ, c))


def along_x(array, step):
    def route(xh, xl):
        place = (2 * xh + xl + step) % 4
        return place // 2, place % 2

    return send(array, ("xh", "xl"), (2, 2), route)


def first_round(block, other):
    chip = jnp.concatenate([block, other], axis=0)
    near, far = along_z(chip, 1), along_z(chip, 2)
    return [block, other, near, far]


def shared(parts, before=None):
    block, other, near, far = parts
    if before is not None:
        passed, _ = lax.optimization_barrier((far, before))
    else:
        passed = far
    return [block, other, near, other_core(near), far, other_core(passed)]


def finished_first(value, before):
    return lax.optimization_barrier((value, before))[0]


def second_round(parts, before=None):
    block, far = parts[0], parts[4]
    third, fourth = along_z(far, 1), along_z(far[: block.shape[0]], 2)
    if before is not None:
        third, fourth, _ = lax.optimization_barrier((third, fourth, before))
    return [third, other_core(third), fourth, other_core(fourth)]


def block_table():
    table = np.zeros((NZ, 2, 2, 2, 24), np.int32)
    for z, xh, xl, c in np.ndindex(NZ, 2, 2, 2):
        away = -1 if c == 0 else 1
        order = [(z, c), (z, 1 - c)]
        for r in range(1, 4):
            order += [(z + away * r, c), (z + away * r, 1 - c)]
            order += [(z - away * r, 1 - c), (z - away * r, c)]
        order += [(z + 4, c), (z + 4, 1 - c)]
        row = [2 * (at % NZ) + core for at, core in order]
        for step in range(4):
            place = (2 * xh + xl + step) % 4
            row.append(2 * (place % 2) + place // 2)
        row.append(int(xh == c))
        table[z, xh, xl, c, : len(row)] = row
    return table.reshape(-1, 24)


def pieces_of(refs):
    rows = min(ref.shape[0] for ref in refs)
    pieces = []
    for ref in refs:
        pieces += [ref[k * rows : (k + 1) * rows, :] for k in range(ref.shape[0] // rows)]
    return pieces


def assemble_body(table, *refs):
    parts, whole = refs[:-1], refs[-1]
    rows = TOKENS // NBLK
    for k, piece in enumerate(pieces_of(parts)):
        at = pl.multiple_of(table[k] * rows, rows)
        for b in range(NBLK):
            whole[b, pl.ds(at, rows), :] = piece[b * rows : (b + 1) * rows, :]


def assemble(table, parts):
    return pl.pallas_call(
        assemble_body,
        out_shape=jax.ShapeDtypeStruct((NBLK, TOKENS, LANE), jnp.bfloat16),
        in_specs=[IN_SMEM] + [IN_VMEM] * len(parts),
        out_specs=IN_VMEM,
        name="assemble",
        cost_estimate=pl.CostEstimate(flops=0, bytes_accessed=4 << 20, transcendentals=0),
        compiler_params=pltpu.CompilerParams(vmem_limit_bytes=24 << 20),
    )(table, *parts)


def in_three(value):
    first = value.astype(jnp.bfloat16)
    rest = value - first.astype(jnp.float32)
    second = rest.astype(jnp.bfloat16)
    third = (rest - second.astype(jnp.float32)).astype(jnp.bfloat16)
    return [first, second, third]


def scale_rows(pieces, gains, at, rows):
    squares = jnp.zeros((TOKENS, LANE), jnp.float32)
    for k, piece in enumerate(pieces):
        wide = piece.astype(jnp.float32)
        squares = squares + wide * wide
        rows[:, k * LANE : (k + 1) * LANE] = (wide * gains[at[k]]).astype(jnp.bfloat16)
    return squares


def fetch_body(layer, natural, table, slots, *refs):
    tiles, matrix, arrived = refs[:-2], refs[-2], refs[-1]
    slot, stays = slots[layer], table[20] == 1
    count = len(tiles) // 2
    for k in range(count):
        mine = slot >= k if k == count - 1 else slot == k
        for moved in range(2):

            @pl.when(jnp.logical_and(mine, jnp.logical_not(stays) if moved else stays))
            def _(tile=tiles[2 * k + moved]):
                for j in range(NBLK):
                    pltpu.make_async_copy(
                        tile.at[j if natural else table[j]], matrix.at[pl.ds(j * LANE, LANE), :], arrived
                    ).start()

    pltpu.make_async_copy(matrix, matrix, arrived).wait()


def fetch(layer, table, slots, tiles):
    flat = [tile for pair in tiles for tile in pair]
    return pl.pallas_call(
        functools.partial(fetch_body, layer, layer == 0),
        out_shape=jax.ShapeDtypeStruct((NBLK * LANE, 512), jnp.bfloat16),
        in_specs=[IN_SMEM] * 2 + [IN_PLACE] * len(flat),
        out_specs=IN_VMEM,
        scratch_shapes=[pltpu.SemaphoreType.DMA],
        name="fetch",
        cost_estimate=pl.CostEstimate(flops=0, bytes_accessed=8 << 20, transcendentals=0),
        compiler_params=pltpu.CompilerParams(vmem_limit_bytes=8 << 20),
    )(table, slots, *flat)


def begin_body(layer, n_parts, table, slots, *refs):
    parts, (gains, matrix, partial, squares, rows) = refs[:n_parts], refs[n_parts:]
    slot = slots[layer]
    order = list(range(NBLK)) if n_parts == 1 else [table[k] for k in range(NBLK)]
    pieces = [parts[0][b] for b in range(EARLY)] if n_parts == 1 else pieces_of(parts)
    squares[...] = scale_rows(pieces, gains, [slot * NBLK + b for b in order[:EARLY]], rows)
    for pair in range(2):
        total = jnp.dot(
            rows[...], matrix[: EARLY * LANE, pair * 256 : (pair + 1) * 256], preferred_element_type=jnp.float32
        )
        partial[2 * pair] = total[:, :LANE]
        partial[2 * pair + 1] = total[:, LANE:]


def begin(layer, table, slots, parts, gains, matrix):
    return pl.pallas_call(
        functools.partial(begin_body, layer, len(parts)),
        out_shape=[
            jax.ShapeDtypeStruct((4, TOKENS, LANE), jnp.float32),
            jax.ShapeDtypeStruct((TOKENS, LANE), jnp.float32),
        ],
        in_specs=[IN_SMEM] * 2 + [IN_VMEM] * (len(parts) + 2),
        out_specs=[IN_VMEM] * 2,
        scratch_shapes=[pltpu.VMEM((TOKENS, EARLY * LANE), jnp.bfloat16)],
        name="begin",
        cost_estimate=pl.CostEstimate(flops=2 * TOKENS * 1280 * 512, bytes_accessed=5 << 20, transcendentals=0),
        compiler_params=pltpu.CompilerParams(vmem_limit_bytes=16 << 20),
    )(table, slots, *parts, gains, matrix)


def finish_body(layer, n_parts, *refs):
    table, slots = refs[:2]
    parts = refs[2 : 2 + n_parts]
    gains, partial, squares, matrix = refs[2 + n_parts : 6 + n_parts]
    sends, own, own_squares, rows, product = refs[6 + n_parts : 9 + n_parts], *refs[9 + n_parts :]
    slot = slots[layer]
    if n_parts == 1:
        pieces, order = [parts[0][b] for b in range(EARLY, NBLK)], range(EARLY, NBLK)
    else:
        pieces, order = pieces_of(parts), [table[k] for k in range(EARLY, NBLK)]
    total = squares[...] + scale_rows(pieces, gains, [slot * NBLK + b for b in order], rows)
    for pair in range(2):
        both = jnp.dot(
            rows[...], matrix[EARLY * LANE :, pair * 256 : (pair + 1) * 256], preferred_element_type=jnp.float32
        )
        product[2 * pair] = both[:, :LANE]
        product[2 * pair + 1] = both[:, LANE:]
    sums = jnp.concatenate(
        [jnp.sum(total[a * LANE : (a + 1) * LANE].T, axis=0, keepdims=True) for a in range(GROUPS)], axis=0
    )
    own_squares[...] = sums
    tail = jnp.concatenate(in_three(sums) + [jnp.zeros((TAIL - 3 * GROUPS, LANE), jnp.bfloat16)], axis=0)
    own[...] = product[table[16]] + partial[table[16]]
    for step in range(1, 4):
        quarter = table[16 + step]
        sends[step - 1][0:TOKENS, :] = (product[quarter] + partial[quarter]).astype(jnp.bfloat16)
        sends[step - 1][TOKENS : TOKENS + TAIL, :] = tail


def finish(layer, table, slots, parts, gains, begun):
    outs = [jax.ShapeDtypeStruct((TOKENS + TAIL, LANE), jnp.bfloat16)] * 3
    outs += [jax.ShapeDtypeStruct((TOKENS, LANE), jnp.float32), jax.ShapeDtypeStruct((GROUPS, LANE), jnp.float32)]
    return pl.pallas_call(
        functools.partial(finish_body, layer, len(parts)),
        out_shape=outs,
        in_specs=[IN_SMEM] * 2 + [IN_VMEM] * (len(parts) + 4),
        out_specs=[IN_VMEM] * 5,
        scratch_shapes=[
            pltpu.VMEM((TOKENS, LATE * LANE), jnp.bfloat16),
            pltpu.VMEM((4, TOKENS, LANE), jnp.float32),
        ],
        name="finish",
        cost_estimate=pl.CostEstimate(flops=2 * TOKENS * 768 * 512, bytes_accessed=5 << 20, transcendentals=0),
        compiler_params=pltpu.CompilerParams(vmem_limit_bytes=24 << 20),
    )(table, slots, *parts, gains, *begun)


def update_body(current, own, own_squares, *refs):
    arrived, result = refs[:3], refs[3]
    total, squares = own[...], own_squares[...]
    for ref in arrived:
        total = total + ref[0:TOKENS, :].astype(jnp.float32)
        tail = ref[TOKENS : TOKENS + TAIL, :].astype(jnp.float32)
        squares = squares + (tail[0:GROUPS] + tail[GROUPS : 2 * GROUPS] + tail[2 * GROUPS : 3 * GROUPS])
    scale = lax.rsqrt(squares * (1.0 / D) + EPSILON)
    column = jnp.concatenate(
        [jnp.broadcast_to(scale[a : a + 1], (LANE, LANE)).T for a in range(GROUPS)], axis=0
    )
    step = (total * column).astype(jnp.bfloat16).astype(jnp.float32)
    result[...] = (current[...].astype(jnp.float32) + step).astype(jnp.bfloat16)


def update(current, own, own_squares, arrived):
    return pl.pallas_call(
        update_body,
        out_shape=jax.ShapeDtypeStruct((TOKENS, LANE), jnp.bfloat16),
        in_specs=[IN_VMEM] * 6,
        out_specs=IN_VMEM,
        name="update",
        cost_estimate=pl.CostEstimate(flops=20 * TOKENS * LANE, bytes_accessed=1 << 20, transcendentals=512),
        compiler_params=pltpu.CompilerParams(vmem_limit_bytes=16 << 20),
    )(current, own, own_squares, *arrived)


def first_gram_body(table, kept, *refs):
    swapped, columns, result, turned, rows, arrived = refs[:PIECES], *refs[PIECES:]
    per = NBLK // PIECES

    @pl.when(table[20] == 1)
    def _():
        pltpu.make_async_copy(kept, rows, arrived).start()

    @pl.when(table[20] == 0)
    def _():
        for k in range(PIECES):
            pltpu.make_async_copy(swapped[k], rows.at[pl.ds(k * per, per)], arrived).start()

    pltpu.make_async_copy(rows, rows, arrived).wait()
    right = columns[...]
    for b in range(NBLK):
        left = rows[b].T
        turned[b * LANE : (b + 1) * LANE, :] = left
        result[b] = jnp.dot(left, right, preferred_element_type=jnp.float32) * (1.0 / TOKENS)


def first_gram(table, kept, swapped, columns):
    return pl.pallas_call(
        first_gram_body,
        out_shape=[
            jax.ShapeDtypeStruct((NBLK, LANE, LANE), jnp.float32),
            jax.ShapeDtypeStruct((NBLK * LANE, TOKENS), jnp.bfloat16),
        ],
        in_specs=[IN_SMEM] + [IN_PLACE] * (1 + PIECES) + [IN_VMEM],
        out_specs=[IN_VMEM] * 2,
        scratch_shapes=[pltpu.VMEM((NBLK, TOKENS, LANE), jnp.bfloat16), pltpu.SemaphoreType.DMA],
        name="first_gram",
        cost_estimate=pl.CostEstimate(flops=2 * TOKENS * 2048 * LANE, bytes_accessed=5 << 20, transcendentals=0),
        compiler_params=pltpu.CompilerParams(vmem_limit_bytes=24 << 20),
    )(table, kept, *swapped, columns)


def gram_body(turned, columns, result):
    total = jnp.dot(turned[...], columns[...], preferred_element_type=jnp.float32)
    result[...] = total.reshape(NBLK, LANE, LANE) * (1.0 / TOKENS)


def gram(turned, columns):
    return pl.pallas_call(
        gram_body,
        out_shape=jax.ShapeDtypeStruct((NBLK, LANE, LANE), jnp.float32),
        in_specs=[IN_VMEM] * 2,
        out_specs=IN_VMEM,
        name="gram",
        cost_estimate=pl.CostEstimate(flops=2 * TOKENS * 2048 * LANE, bytes_accessed=3 << 20, transcendentals=0),
        compiler_params=pltpu.CompilerParams(vmem_limit_bytes=16 << 20),
    )(turned, columns)


def to_other_core_of_chip(here):
    beside = send(here, ("y", "xl", "c"), (NY, 2, 2), lambda y, xl, c: (y, xl, 1 - c) if c == y % 2 else None)
    return jnp.where(lax.axis_index("c") == lax.axis_index("y") % 2, here, beside)


def quarter_of_section(block):
    own_quarter = 2 * lax.axis_index("xl") + lax.axis_index("c") == lax.axis_index("y")
    across = send(
        block, ("y", "xl", "c"), (NY, 2, 2), lambda y, xl, c: (y, 1 - xl, c) if 2 * xl + c == y else None
    )
    return to_other_core_of_chip(jnp.where(own_quarter, block, across))


def local(block_in, weights, gains, layer_counts):
    section = lax.axis_index("y")
    sections = jnp.arange(NY, dtype=jnp.int32)
    start = jnp.sum(jnp.where(sections < section, layer_counts, 0))
    layers = jnp.arange(LAYERS, dtype=jnp.int32)
    slots = jnp.clip(layers - start, 0, SLOTS - 1)
    ends = jnp.sum(jnp.where(sections[None, :] <= sections[:3, None], layer_counts[None, :], 0), axis=1)
    hops = jnp.any(ends[:, None] == layers[None, :] + 1, axis=0)
    table = lax.dynamic_index_in_dim(
        jnp.asarray(block_table()), lax.axis_index(("z", "xh", "xl", "c")), 0, keepdims=False
    )

    stays = lax.axis_index("xh") == lax.axis_index("c")
    by_block = block_in.transpose(1, 0, 2).reshape(TOKENS, LANE)
    mine = jnp.where(stays, by_block, swap_roles(by_block))
    gains = gains.reshape(SLOTS * NBLK, 1, LANE)
    gains = jnp.where(stays, gains, swap_roles(gains))

    def tile(slot, early, after):
        kept = finished_first(weights, early)[slot]
        return kept, swap_roles(finished_first(kept, after))

    other = other_core(mine)
    early = shared(first_round(mine, other))
    tiles = [tile(0, mine, other)]
    whole = assemble(table, early + second_round(early))
    current = lax.dynamic_index_in_dim(
        whole, 2 * lax.axis_index("z") + lax.axis_index("c"), 0, keepdims=False
    )
    first, turned, swapped = current, None, []
    for layer in range(LAYERS):
        if layer:
            other = other_core(current)
            matrix = fetch(layer, table, finished_first(slots, other), tiles)
            early = shared(first_round(current, other), matrix)
            begun = begin(
                layer, table, slots if turned is None else finished_first(slots, turned), early, gains, matrix
            )
            before = [begun[1]]
            if len(tiles) == SLOTS and len(swapped) < PIECES and layer >= SLOTS:
                per = NBLK // PIECES
                piece = finished_first(whole, matrix)[len(swapped) * per : (len(swapped) + 1) * per]
                swapped.append(swap_roles(piece))
                before.append(swapped[-1])
            if layer == LAYERS - 2:
                first = jnp.where(stays, first, swap_roles(finished_first(first, matrix)))
                columns = quarter_of_section(first)
                before.append(columns)
            late = second_round(early, before)
        else:
            matrix = fetch(layer, table, slots, tiles)
            early = late = [whole]
            begun = begin(layer, table, slots, early, gains, matrix)
        outs = finish(layer, table, slots, late, gains, [*begun, matrix])
        arrived = [along_x(outs[k], k + 1) for k in range(3)]
        current = update(current, outs[3], outs[4], arrived)
        if layer < SLOTS - 1:
            tiles.append(tile(layer + 1, outs[4], current))
        if layer == LAYERS - 2:
            gram_in, turned = first_gram(table, whole, swapped, columns)
        if layer < LAYERS - 1:
            current = lax.cond(
                hops[layer],
                lambda v: send(v, ("y",), (NY,), lambda y: (y + 1,) if y < NY - 1 else None),
                lambda v: v,
                current,
            )

    def from_last(array, target):
        return send(
            array,
            ("xh", "y", "xl", "c"),
            (2, NY, 2, 2),
            lambda xh, y, xl, c: target(xh, xl, c) if y == NY - 1 else None,
        )

    by_tokens = lax.all_to_all(current.reshape(NBLK, TOKENS // NBLK, LANE), ("z", "c"), 0, 0, tiled=True)
    straight = from_last(current, lambda xh, xl, c: (c, 2 * xl + xh, xl, xh))
    across = from_last(current, lambda xh, xl, c: (c, 2 * xl + xh, 1 - xl, xh))
    own_quarter = 2 * lax.axis_index("xl") + lax.axis_index("c") == section
    gram_cross = gram(turned, to_other_core_of_chip(jnp.where(own_quarter, straight, across)))
    copies = [from_last(by_tokens, lambda xh, xl, c, plane=plane: (c, plane, xl, xh)) for plane in range(NY)]
    copies = finished_first(copies, gram_cross)
    block_out = copies[0]
    for plane in range(1, NY):
        block_out = jnp.where(section == plane, copies[plane], block_out)
    shape = (NBLK, LANE, 1, LANE)
    return block_out.transpose(1, 0, 2), gram_in.reshape(shape), gram_cross.reshape(shape)


def solution(mesh):
    finer = Mesh(mesh.devices.reshape(NZ, 2, NY, 2, 2), AXES)
    dp, section, tensor = ("z", "xh"), "y", ("xl", "c")
    return jax.shard_map(
        local,
        mesh=finer,
        in_specs=(P(dp, None, tensor), P(section, None, tensor, dp), P(section, None, tensor), P()),
        out_specs=(P(dp, None, tensor), P(None, tensor, dp, section), P(None, tensor, dp, section)),
        check_vma=False,
    )
```

```python
import functools
import jax
import jax.numpy as jnp
import numpy as np
from jax import lax
from jax.experimental import pallas as pl
from jax.experimental.pallas import tpu as pltpu
from jax.sharding import Mesh, PartitionSpec as P

D = 8192
SLOTS = 3
LAYERS = 8
TOKENS = 512
NBLK = 16
LANE = 128
NZ = 8
NY = 4
EPSILON = 1e-05
TAIL = 16
GROUPS = TOKENS // LANE
EARLY = 10
PIECES = 4
LATE = NBLK - EARLY
AXES = ("z", "xh", "y", "xl", "c")
IN_VMEM = pl.BlockSpec(memory_space=pltpu.VMEM)
IN_SMEM = pl.BlockSpec(memory_space=pltpu.SMEM)
IN_PLACE = pl.BlockSpec(memory_space=pltpu.HBM)


def send(array, axes, sizes, route):
    pairs = []
    for source in np.ndindex(*sizes):
        target = route(*source)
        if target is not None:
            pairs.append((int(np.ravel_multi_index(source, sizes)), int(np.ravel_multi_index(target, sizes))))
    return lax.ppermute(array, axes, pairs)


def swap_roles(array):
    return send(array, ("xh", "c"), (2, 2), lambda xh, c: (c, xh) if xh != c else None)


def other_core(array):
    return send(array, ("c",), (2,), lambda c: (1 - c,))


def along_z(array, distance):
    return send(array, ("z", "c"), (NZ, 2), lambda z, c: ((z + distance * (1 - 2 * c)) % NZ, c))


def along_x(array, step):
    def route(xh, xl):
        place = (2 * xh + xl + step) % 4
        return place // 2, place % 2

    return send(array, ("xh", "xl"), (2, 2), route)


def first_round(block, other):
    chip = jnp.concatenate([block, other], axis=0)
    near, far = along_z(chip, 1), along_z(chip, 2)
    return [block, other, near, far]


def shared(parts, before=None):
    block, other, near, far = parts
    if before is not None:
        passed, _ = lax.optimization_barrier((far, before))
    else:
        passed = far
    return [block, other, near, other_core(near), far, other_core(passed)]


def finished_first(value, before):
    return lax.optimization_barrier((value, before))[0]


def second_round(parts, before=None):
    block, far = parts[0], parts[4]
    third, fourth = along_z(far, 1), along_z(far[: block.shape[0]], 2)
    if before is not None:
        third, fourth, _ = lax.optimization_barrier((third, fourth, before))
    return [third, other_core(third), fourth, other_core(fourth)]


def block_table():
    table = np.zeros((NZ, 2, 2, 2, 40), np.int32)
    for z, xh, xl, c in np.ndindex(NZ, 2, 2, 2):
        away = -1 if c == 0 else 1
        order = [(z, c), (z, 1 - c)]
        for r in range(1, 4):
            order += [(z + away * r, c), (z + away * r, 1 - c)]
            order += [(z - away * r, 1 - c), (z - away * r, c)]
        order += [(z + 4, c), (z + 4, 1 - c)]
        row = [2 * (at % NZ) + core for at, core in order]
        for step in range(4):
            place = (2 * xh + xl + step) % 4
            row.append(2 * (place % 2) + place // 2)
        row.append(int(xh == c))
        table[z, xh, xl, c, : len(row)] = row
        table[z, xh, xl, c, 24:] = np.argsort(row[:NBLK])
    return table.reshape(-1, 40)


def pieces_of(refs):
    rows = min(ref.shape[0] for ref in refs)
    pieces = []
    for ref in refs:
        pieces += [ref[k * rows : (k + 1) * rows, :] for k in range(ref.shape[0] // rows)]
    return pieces


def assemble_body(table, *refs):
    parts, whole = refs[:-1], refs[-1]
    rows = TOKENS // NBLK
    for k, piece in enumerate(pieces_of(parts)):
        at = pl.multiple_of(table[k] * rows, rows)
        for b in range(NBLK):
            whole[b, pl.ds(at, rows), :] = piece[b * rows : (b + 1) * rows, :]


def assemble(table, parts):
    return pl.pallas_call(
        assemble_body,
        out_shape=jax.ShapeDtypeStruct((NBLK, TOKENS, LANE), jnp.bfloat16),
        in_specs=[IN_SMEM] + [IN_VMEM] * len(parts),
        out_specs=IN_VMEM,
        name="assemble",
        cost_estimate=pl.CostEstimate(flops=0, bytes_accessed=4 << 20, transcendentals=0),
        compiler_params=pltpu.CompilerParams(vmem_limit_bytes=24 << 20),
    )(table, *parts)


def in_three(value):
    first = value.astype(jnp.bfloat16)
    rest = value - first.astype(jnp.float32)
    second = rest.astype(jnp.bfloat16)
    third = (rest - second.astype(jnp.float32)).astype(jnp.bfloat16)
    return [first, second, third]


def scale_rows(pieces, gains, at, rows):
    squares = jnp.zeros((TOKENS, LANE), jnp.float32)
    for k, piece in enumerate(pieces):
        wide = piece.astype(jnp.float32)
        squares = squares + wide * wide
        rows[:, k * LANE : (k + 1) * LANE] = (wide * gains[at[k]]).astype(jnp.bfloat16)
    return squares


def fetch_body(layer, natural, counts, table, slots, *refs):
    pieces, matrix, arrived = list(refs[:-2]), refs[-2], refs[-1]
    slot, stays = slots[layer], table[20] == 1
    for k, count in enumerate(counts):
        mine = slot >= k if k == len(counts) - 1 else slot == k
        for moved in range(2):
            chosen = [pieces.pop(0) for _ in range(count)]

            @pl.when(jnp.logical_and(mine, jnp.logical_not(stays) if moved else stays))
            def _(chosen=chosen):
                per = NBLK // len(chosen)
                for b in range(NBLK):
                    at = b if natural else table[24 + b]
                    pltpu.make_async_copy(
                        chosen[b // per].at[b % per], matrix.at[pl.ds(pl.multiple_of(at * LANE, LANE), LANE), :], arrived
                    ).start()

    pltpu.make_async_copy(matrix, matrix, arrived).wait()


def fetch(layer, table, slots, tiles):
    flat, counts = [], []
    for pieces in tiles:
        flat += [own for own, _ in pieces] + [moved for _, moved in pieces]
        counts.append(len(pieces))
    return pl.pallas_call(
        functools.partial(fetch_body, layer, layer == 0, counts),
        out_shape=jax.ShapeDtypeStruct((NBLK * LANE, 512), jnp.bfloat16),
        in_specs=[IN_SMEM] * 2 + [IN_PLACE] * len(flat),
        out_specs=IN_VMEM,
        scratch_shapes=[pltpu.SemaphoreType.DMA],
        name="fetch",
        cost_estimate=pl.CostEstimate(flops=0, bytes_accessed=8 << 20, transcendentals=0),
        compiler_params=pltpu.CompilerParams(vmem_limit_bytes=8 << 20),
    )(table, slots, *flat)


def begin_body(layer, n_parts, table, slots, *refs):
    parts, (gains, matrix, partial, squares, rows) = refs[:n_parts], refs[n_parts:]
    slot = slots[layer]
    order = list(range(NBLK)) if n_parts == 1 else [table[k] for k in range(NBLK)]
    pieces = [parts[0][b] for b in range(EARLY)] if n_parts == 1 else pieces_of(parts)
    squares[...] = scale_rows(pieces, gains, [slot * NBLK + b for b in order[:EARLY]], rows)
    for pair in range(2):
        total = jnp.dot(
            rows[...], matrix[: EARLY * LANE, pair * 256 : (pair + 1) * 256], preferred_element_type=jnp.float32
        )
        partial[2 * pair] = total[:, :LANE]
        partial[2 * pair + 1] = total[:, LANE:]


def begin(layer, table, slots, parts, gains, matrix):
    return pl.pallas_call(
        functools.partial(begin_body, layer, len(parts)),
        out_shape=[
            jax.ShapeDtypeStruct((4, TOKENS, LANE), jnp.float32),
            jax.ShapeDtypeStruct((TOKENS, LANE), jnp.float32),
        ],
        in_specs=[IN_SMEM] * 2 + [IN_VMEM] * (len(parts) + 2),
        out_specs=[IN_VMEM] * 2,
        scratch_shapes=[pltpu.VMEM((TOKENS, EARLY * LANE), jnp.bfloat16)],
        name="begin",
        cost_estimate=pl.CostEstimate(flops=2 * TOKENS * 1280 * 512, bytes_accessed=5 << 20, transcendentals=0),
        compiler_params=pltpu.CompilerParams(vmem_limit_bytes=16 << 20),
    )(table, slots, *parts, gains, matrix)


def finish_body(layer, n_parts, *refs):
    table, slots = refs[:2]
    parts = refs[2 : 2 + n_parts]
    gains, partial, squares, matrix = refs[2 + n_parts : 6 + n_parts]
    sends, own, own_squares, rows, product = refs[6 + n_parts : 9 + n_parts], *refs[9 + n_parts :]
    slot = slots[layer]
    if n_parts == 1:
        pieces, order = [parts[0][b] for b in range(EARLY, NBLK)], range(EARLY, NBLK)
    else:
        pieces, order = pieces_of(parts), [table[k] for k in range(EARLY, NBLK)]
    total = squares[...] + scale_rows(pieces, gains, [slot * NBLK + b for b in order], rows)
    for pair in range(2):
        both = jnp.dot(
            rows[...], matrix[EARLY * LANE :, pair * 256 : (pair + 1) * 256], preferred_element_type=jnp.float32
        )
        product[2 * pair] = both[:, :LANE]
        product[2 * pair + 1] = both[:, LANE:]
    sums = jnp.concatenate(
        [jnp.sum(total[a * LANE : (a + 1) * LANE].T, axis=0, keepdims=True) for a in range(GROUPS)], axis=0
    )
    own_squares[...] = sums
    tail = jnp.concatenate(in_three(sums) + [jnp.zeros((TAIL - 3 * GROUPS, LANE), jnp.bfloat16)], axis=0)
    own[...] = product[table[16]] + partial[table[16]]
    for step in range(1, 4):
        quarter = table[16 + step]
        sends[step - 1][0:TOKENS, :] = (product[quarter] + partial[quarter]).astype(jnp.bfloat16)
        sends[step - 1][TOKENS : TOKENS + TAIL, :] = tail


def finish(layer, table, slots, parts, gains, begun):
    outs = [jax.ShapeDtypeStruct((TOKENS + TAIL, LANE), jnp.bfloat16)] * 3
    outs += [jax.ShapeDtypeStruct((TOKENS, LANE), jnp.float32), jax.ShapeDtypeStruct((GROUPS, LANE), jnp.float32)]
    return pl.pallas_call(
        functools.partial(finish_body, layer, len(parts)),
        out_shape=outs,
        in_specs=[IN_SMEM] * 2 + [IN_VMEM] * (len(parts) + 4),
        out_specs=[IN_VMEM] * 5,
        scratch_shapes=[
            pltpu.VMEM((TOKENS, LATE * LANE), jnp.bfloat16),
            pltpu.VMEM((4, TOKENS, LANE), jnp.float32),
        ],
        name="finish",
        cost_estimate=pl.CostEstimate(flops=2 * TOKENS * 768 * 512, bytes_accessed=5 << 20, transcendentals=0),
        compiler_params=pltpu.CompilerParams(vmem_limit_bytes=24 << 20),
    )(table, slots, *parts, gains, *begun)


def update_body(current, own, own_squares, *refs):
    arrived, result = refs[:3], refs[3]
    total, squares = own[...], own_squares[...]
    for ref in arrived:
        total = total + ref[0:TOKENS, :].astype(jnp.float32)
        tail = ref[TOKENS : TOKENS + TAIL, :].astype(jnp.float32)
        squares = squares + (tail[0:GROUPS] + tail[GROUPS : 2 * GROUPS] + tail[2 * GROUPS : 3 * GROUPS])
    scale = lax.rsqrt(squares * (1.0 / D) + EPSILON)
    column = jnp.concatenate(
        [jnp.broadcast_to(scale[a : a + 1], (LANE, LANE)).T for a in range(GROUPS)], axis=0
    )
    step = (total * column).astype(jnp.bfloat16).astype(jnp.float32)
    result[...] = (current[...].astype(jnp.float32) + step).astype(jnp.bfloat16)


def update(current, own, own_squares, arrived):
    return pl.pallas_call(
        update_body,
        out_shape=jax.ShapeDtypeStruct((TOKENS, LANE), jnp.bfloat16),
        in_specs=[IN_VMEM] * 6,
        out_specs=IN_VMEM,
        name="update",
        cost_estimate=pl.CostEstimate(flops=20 * TOKENS * LANE, bytes_accessed=1 << 20, transcendentals=512),
        compiler_params=pltpu.CompilerParams(vmem_limit_bytes=16 << 20),
    )(current, own, own_squares, *arrived)


def first_gram_body(table, kept, *refs):
    swapped, columns, result, turned, rows, arrived = refs[:PIECES], *refs[PIECES:]
    per = NBLK // PIECES

    @pl.when(table[20] == 1)
    def _():
        pltpu.make_async_copy(kept, rows, arrived).start()

    @pl.when(table[20] == 0)
    def _():
        for k in range(PIECES):
            pltpu.make_async_copy(swapped[k], rows.at[pl.ds(k * per, per)], arrived).start()

    pltpu.make_async_copy(rows, rows, arrived).wait()
    right = columns[...]
    for b in range(NBLK):
        left = rows[b].T
        turned[b * LANE : (b + 1) * LANE, :] = left
        result[b] = jnp.dot(left, right, preferred_element_type=jnp.float32) * (1.0 / TOKENS)


def first_gram(table, kept, swapped, columns):
    return pl.pallas_call(
        first_gram_body,
        out_shape=[
            jax.ShapeDtypeStruct((NBLK, LANE, LANE), jnp.float32),
            jax.ShapeDtypeStruct((NBLK * LANE, TOKENS), jnp.bfloat16),
        ],
        in_specs=[IN_SMEM] + [IN_PLACE] * (1 + PIECES) + [IN_VMEM],
        out_specs=[IN_VMEM] * 2,
        scratch_shapes=[pltpu.VMEM((NBLK, TOKENS, LANE), jnp.bfloat16), pltpu.SemaphoreType.DMA],
        name="first_gram",
        cost_estimate=pl.CostEstimate(flops=2 * TOKENS * 2048 * LANE, bytes_accessed=5 << 20, transcendentals=0),
        compiler_params=pltpu.CompilerParams(vmem_limit_bytes=24 << 20),
    )(table, kept, *swapped, columns)


def gram_body(turned, columns, result):
    total = jnp.dot(turned[...], columns[...], preferred_element_type=jnp.float32)
    result[...] = total.reshape(NBLK, LANE, LANE) * (1.0 / TOKENS)


def gram(turned, columns):
    return pl.pallas_call(
        gram_body,
        out_shape=jax.ShapeDtypeStruct((NBLK, LANE, LANE), jnp.float32),
        in_specs=[IN_VMEM] * 2,
        out_specs=IN_VMEM,
        name="gram",
        cost_estimate=pl.CostEstimate(flops=2 * TOKENS * 2048 * LANE, bytes_accessed=3 << 20, transcendentals=0),
        compiler_params=pltpu.CompilerParams(vmem_limit_bytes=16 << 20),
    )(turned, columns)


def to_other_core_of_chip(here):
    beside = send(here, ("y", "xl", "c"), (NY, 2, 2), lambda y, xl, c: (y, xl, 1 - c) if c == y % 2 else None)
    return jnp.where(lax.axis_index("c") == lax.axis_index("y") % 2, here, beside)


def to_chip_across(block):
    own_quarter = 2 * lax.axis_index("xl") + lax.axis_index("c") == lax.axis_index("y")
    across = send(
        block, ("y", "xl", "c"), (NY, 2, 2), lambda y, xl, c: (y, 1 - xl, c) if 2 * xl + c == y else None
    )
    return jnp.where(own_quarter, block, across)


def local(block_in, weights, gains, layer_counts):
    section = lax.axis_index("y")
    sections = jnp.arange(NY, dtype=jnp.int32)
    start = jnp.sum(jnp.where(sections < section, layer_counts, 0))
    layers = jnp.arange(LAYERS, dtype=jnp.int32)
    slots = jnp.clip(layers - start, 0, SLOTS - 1)
    ends = jnp.sum(jnp.where(sections[None, :] <= sections[:3, None], layer_counts[None, :], 0), axis=1)
    hops = jnp.any(ends[:, None] == layers[None, :] + 1, axis=0)
    table = lax.dynamic_index_in_dim(
        jnp.asarray(block_table()), lax.axis_index(("z", "xh", "xl", "c")), 0, keepdims=False
    )

    stays = lax.axis_index("xh") == lax.axis_index("c")
    by_block = block_in.transpose(1, 0, 2).reshape(TOKENS, LANE)
    mine = jnp.where(stays, by_block, swap_roles(by_block))
    gains = gains.reshape(SLOTS * NBLK, 1, LANE)
    gains = jnp.where(stays, gains, swap_roles(gains))

    def piece(slot, first, count, early, after=None):
        kept = finished_first(weights, early)[slot, first : first + count]
        return kept, swap_roles(kept if after is None else finished_first(kept, after))

    other = other_core(mine)
    early = shared(first_round(mine, other))
    tiles = [[piece(0, 0, NBLK, mine, other)]]
    whole = assemble(table, early + second_round(early))
    current = lax.dynamic_index_in_dim(
        whole, 2 * lax.axis_index("z") + lax.axis_index("c"), 0, keepdims=False
    )
    first, turned, swapped = current, None, []
    for layer in range(LAYERS):
        if layer:
            other = other_core(current)
            matrix = fetch(layer, table, finished_first(slots, other), tiles)
            early = shared(first_round(current, other), matrix)
            begun = begin(
                layer, table, slots if turned is None else finished_first(slots, turned), early, gains, matrix
            )
            before = [begun[1]]
            if layer == 1:
                pieces = [piece(2, 4 * k, 4, matrix) for k in range(2)]
                before += [moved for _, moved in pieces]
                pieces.append(piece(2, 8, 4, begun[1]))
            if len(tiles) == SLOTS and len(swapped) < PIECES and layer >= SLOTS:
                per = NBLK // PIECES
                part = finished_first(whole, matrix)[len(swapped) * per : (len(swapped) + 1) * per]
                swapped.append(swap_roles(part))
                before.append(swapped[-1])
            if layer == LAYERS - 4:
                first = jnp.where(stays, first, swap_roles(finished_first(first, matrix)))
                before.append(first)
            if layer == LAYERS - 3:
                columns = to_chip_across(finished_first(first, matrix))
                before.append(columns)
            if layer == LAYERS - 2:
                columns = to_other_core_of_chip(finished_first(columns, matrix))
                before.append(columns)
            late = second_round(early, before)
        else:
            matrix = fetch(layer, table, slots, tiles)
            early = late = [whole]
            begun = begin(layer, table, slots, early, gains, matrix)
        outs = finish(layer, table, slots, late, gains, [*begun, matrix])
        arrived = [along_x(outs[k], k + 1) for k in range(3)]
        current = update(current, outs[3], outs[4], arrived)
        if layer == 0:
            tiles.append([piece(1, 0, NBLK, outs[4], current)])
        if layer == 1:
            tiles.append(pieces + [piece(2, 12, 4, outs[4])])
        if layer == LAYERS - 2:
            gram_in, turned = first_gram(table, whole, swapped, columns)
        if layer < LAYERS - 1:
            current = lax.cond(
                hops[layer],
                lambda v: send(v, ("y",), (NY,), lambda y: (y + 1,) if y < NY - 1 else None),
                lambda v: v,
                current,
            )

    def from_last(array, target):
        return send(
            array,
            ("xh", "y", "xl", "c"),
            (2, NY, 2, 2),
            lambda xh, y, xl, c: target(xh, xl, c) if y == NY - 1 else None,
        )

    by_tokens = lax.all_to_all(current.reshape(NBLK, TOKENS // NBLK, LANE), ("z", "c"), 0, 0, tiled=True)
    straight = from_last(current, lambda xh, xl, c: (c, 2 * xl + xh, xl, xh))
    across = from_last(current, lambda xh, xl, c: (c, 2 * xl + xh, 1 - xl, xh))
    own_quarter = 2 * lax.axis_index("xl") + lax.axis_index("c") == section
    gram_cross = gram(turned, to_other_core_of_chip(jnp.where(own_quarter, straight, across)))
    copies = [from_last(by_tokens, lambda xh, xl, c, plane=plane: (c, plane, xl, xh)) for plane in range(NY)]
    copies = finished_first(copies, gram_cross)
    block_out = copies[0]
    for plane in range(1, NY):
        block_out = jnp.where(section == plane, copies[plane], block_out)
    shape = (NBLK, LANE, 1, LANE)
    return block_out.transpose(1, 0, 2), gram_in.reshape(shape), gram_cross.reshape(shape)


def solution(mesh):
    finer = Mesh(mesh.devices.reshape(NZ, 2, NY, 2, 2), AXES)
    dp, section, tensor = ("z", "xh"), "y", ("xl", "c")
    return jax.shard_map(
        local,
        mesh=finer,
        in_specs=(P(dp, None, tensor), P(section, None, tensor, dp), P(section, None, tensor), P()),
        out_specs=(P(dp, None, tensor), P(None, tensor, dp, section), P(None, tensor, dp, section)),
        check_vma=False,
    )
```

```python
import functools
import jax
import jax.numpy as jnp
import numpy as np
from jax import lax
from jax.experimental import pallas as pl
from jax.experimental.pallas import tpu as pltpu
from jax.sharding import Mesh, PartitionSpec as P

D = 8192
SLOTS = 3
LAYERS = 8
TOKENS = 512
NBLK = 16
LANE = 128
NZ = 8
NY = 4
EPSILON = 1e-05
TAIL = 16
GROUPS = TOKENS // LANE
EARLY = 10
LATE = NBLK - EARLY
AXES = ("z", "xh", "y", "xl", "c")
IN_VMEM = pl.BlockSpec(memory_space=pltpu.VMEM)
IN_SMEM = pl.BlockSpec(memory_space=pltpu.SMEM)
IN_PLACE = pl.BlockSpec(memory_space=pltpu.HBM)


def send(array, axes, sizes, route):
    pairs = []
    for source in np.ndindex(*sizes):
        target = route(*source)
        if target is not None:
            pairs.append((int(np.ravel_multi_index(source, sizes)), int(np.ravel_multi_index(target, sizes))))
    return lax.ppermute(array, axes, pairs)


def swap_roles(array):
    return send(array, ("xh", "c"), (2, 2), lambda xh, c: (c, xh) if xh != c else None)


def other_core(array):
    return send(array, ("c",), (2,), lambda c: (1 - c,))


def along_z(array, distance):
    return send(array, ("z", "c"), (NZ, 2), lambda z, c: ((z + distance * (1 - 2 * c)) % NZ, c))


def along_x(array, step):
    def route(xh, xl):
        place = (2 * xh + xl + step) % 4
        return place // 2, place % 2

    return send(array, ("xh", "xl"), (2, 2), route)


def first_round(block, other):
    chip = jnp.concatenate([block, other], axis=0)
    near, far = along_z(chip, 1), along_z(chip, 2)
    return [block, other, near, far]


def shared(parts, before=None):
    block, other, near, far = parts
    if before is not None:
        passed, _ = lax.optimization_barrier((far, before))
    else:
        passed = far
    return [block, other, near, other_core(near), far, other_core(passed)]


def finished_first(value, before):
    return lax.optimization_barrier((value, before))[0]


def second_round(parts, before=None):
    block, far = parts[0], parts[4]
    third, fourth = along_z(far, 1), along_z(far[: block.shape[0]], 2)
    if before is not None:
        third, fourth, _ = lax.optimization_barrier((third, fourth, before))
    return [third, other_core(third), fourth, other_core(fourth)]


def block_table():
    table = np.zeros((NZ, 2, 2, 2, 24), np.int32)
    for z, xh, xl, c in np.ndindex(NZ, 2, 2, 2):
        away = -1 if c == 0 else 1
        order = [(z, c), (z, 1 - c)]
        for r in range(1, 4):
            order += [(z + away * r, c), (z + away * r, 1 - c)]
            order += [(z - away * r, 1 - c), (z - away * r, c)]
        order += [(z + 4, c), (z + 4, 1 - c)]
        row = [2 * (at % NZ) + core for at, core in order]
        for step in range(4):
            place = (2 * xh + xl + step) % 4
            row.append(2 * (place % 2) + place // 2)
        row.append(int(xh == c))
        table[z, xh, xl, c, : len(row)] = row
    return table.reshape(-1, 24)


def pieces_of(refs):
    rows = min(ref.shape[0] for ref in refs)
    pieces = []
    for ref in refs:
        pieces += [ref[k * rows : (k + 1) * rows, :] for k in range(ref.shape[0] // rows)]
    return pieces


def assemble_body(table, *refs):
    parts, whole = refs[:-1], refs[-1]
    rows = TOKENS // NBLK
    for k, piece in enumerate(pieces_of(parts)):
        at = pl.multiple_of(table[k] * rows, rows)
        for b in range(NBLK):
            whole[b, pl.ds(at, rows), :] = piece[b * rows : (b + 1) * rows, :]


def assemble(table, parts):
    return pl.pallas_call(
        assemble_body,
        out_shape=jax.ShapeDtypeStruct((NBLK, TOKENS, LANE), jnp.bfloat16),
        in_specs=[IN_SMEM] + [IN_VMEM] * len(parts),
        out_specs=IN_VMEM,
        name="assemble",
        cost_estimate=pl.CostEstimate(flops=0, bytes_accessed=4 << 20, transcendentals=0),
        compiler_params=pltpu.CompilerParams(vmem_limit_bytes=24 << 20),
    )(table, *parts)


def in_three(value):
    first = value.astype(jnp.bfloat16)
    rest = value - first.astype(jnp.float32)
    second = rest.astype(jnp.bfloat16)
    third = (rest - second.astype(jnp.float32)).astype(jnp.bfloat16)
    return [first, second, third]


def scale_rows(pieces, gains, at, rows):
    squares = jnp.zeros((TOKENS, LANE), jnp.float32)
    for k, piece in enumerate(pieces):
        wide = piece.astype(jnp.float32)
        squares = squares + wide * wide
        rows[:, k * LANE : (k + 1) * LANE] = (wide * gains[at[k]]).astype(jnp.bfloat16)
    return squares


def fetch_body(layer, natural, table, slots, *refs):
    tiles, matrix, arrived = refs[:-2], refs[-2], refs[-1]
    slot, stays = slots[layer], table[20] == 1
    count = len(tiles) // 2
    for k in range(count):
        mine = slot >= k if k == count - 1 else slot == k
        for moved in range(2):

            @pl.when(jnp.logical_and(mine, jnp.logical_not(stays) if moved else stays))
            def _(tile=tiles[2 * k + moved]):
                for j in range(NBLK):
                    pltpu.make_async_copy(
                        tile.at[j if natural else table[j]], matrix.at[pl.ds(j * LANE, LANE), :], arrived
                    ).start()

    pltpu.make_async_copy(matrix, matrix, arrived).wait()


def fetch(layer, table, slots, tiles):
    flat = [tile for pair in tiles for tile in pair]
    return pl.pallas_call(
        functools.partial(fetch_body, layer, layer == 0),
        out_shape=jax.ShapeDtypeStruct((NBLK * LANE, 512), jnp.bfloat16),
        in_specs=[IN_SMEM] * 2 + [IN_PLACE] * len(flat),
        out_specs=IN_VMEM,
        scratch_shapes=[pltpu.SemaphoreType.DMA],
        name="fetch",
        cost_estimate=pl.CostEstimate(flops=0, bytes_accessed=8 << 20, transcendentals=0),
        compiler_params=pltpu.CompilerParams(vmem_limit_bytes=8 << 20),
    )(table, slots, *flat)


def begin_body(layer, n_parts, table, slots, *refs):
    parts, (gains, matrix, partial, squares, rows) = refs[:n_parts], refs[n_parts:]
    slot = slots[layer]
    order = list(range(NBLK)) if n_parts == 1 else [table[k] for k in range(NBLK)]
    pieces = [parts[0][b] for b in range(EARLY)] if n_parts == 1 else pieces_of(parts)
    squares[...] = scale_rows(pieces, gains, [slot * NBLK + b for b in order[:EARLY]], rows)
    for pair in range(2):
        total = jnp.dot(
            rows[...], matrix[: EARLY * LANE, pair * 256 : (pair + 1) * 256], preferred_element_type=jnp.float32
        )
        partial[2 * pair] = total[:, :LANE]
        partial[2 * pair + 1] = total[:, LANE:]


def begin(layer, table, slots, parts, gains, matrix):
    return pl.pallas_call(
        functools.partial(begin_body, layer, len(parts)),
        out_shape=[
            jax.ShapeDtypeStruct((4, TOKENS, LANE), jnp.float32),
            jax.ShapeDtypeStruct((TOKENS, LANE), jnp.float32),
        ],
        in_specs=[IN_SMEM] * 2 + [IN_VMEM] * (len(parts) + 2),
        out_specs=[IN_VMEM] * 2,
        scratch_shapes=[pltpu.VMEM((TOKENS, EARLY * LANE), jnp.bfloat16)],
        name="begin",
        cost_estimate=pl.CostEstimate(flops=2 * TOKENS * 1280 * 512, bytes_accessed=5 << 20, transcendentals=0),
        compiler_params=pltpu.CompilerParams(vmem_limit_bytes=16 << 20),
    )(table, slots, *parts, gains, matrix)


def finish_body(layer, n_parts, *refs):
    table, slots = refs[:2]
    parts = refs[2 : 2 + n_parts]
    gains, partial, squares, matrix = refs[2 + n_parts : 6 + n_parts]
    sends, own, own_squares, rows, product = refs[6 + n_parts : 9 + n_parts], *refs[9 + n_parts :]
    slot = slots[layer]
    if n_parts == 1:
        pieces, order = [parts[0][b] for b in range(EARLY, NBLK)], range(EARLY, NBLK)
    else:
        pieces, order = pieces_of(parts), [table[k] for k in range(EARLY, NBLK)]
    total = squares[...] + scale_rows(pieces, gains, [slot * NBLK + b for b in order], rows)
    for pair in range(2):
        both = jnp.dot(
            rows[...], matrix[EARLY * LANE :, pair * 256 : (pair + 1) * 256], preferred_element_type=jnp.float32
        )
        product[2 * pair] = both[:, :LANE]
        product[2 * pair + 1] = both[:, LANE:]
    sums = jnp.concatenate(
        [jnp.sum(total[a * LANE : (a + 1) * LANE].T, axis=0, keepdims=True) for a in range(GROUPS)], axis=0
    )
    own_squares[...] = sums
    tail = jnp.concatenate(in_three(sums) + [jnp.zeros((TAIL - 3 * GROUPS, LANE), jnp.bfloat16)], axis=0)
    own[...] = product[table[16]] + partial[table[16]]
    for step in range(1, 4):
        quarter = table[16 + step]
        sends[step - 1][0:TOKENS, :] = (product[quarter] + partial[quarter]).astype(jnp.bfloat16)
        sends[step - 1][TOKENS : TOKENS + TAIL, :] = tail


def finish(layer, table, slots, parts, gains, begun):
    outs = [jax.ShapeDtypeStruct((TOKENS + TAIL, LANE), jnp.bfloat16)] * 3
    outs += [jax.ShapeDtypeStruct((TOKENS, LANE), jnp.float32), jax.ShapeDtypeStruct((GROUPS, LANE), jnp.float32)]
    return pl.pallas_call(
        functools.partial(finish_body, layer, len(parts)),
        out_shape=outs,
        in_specs=[IN_SMEM] * 2 + [IN_VMEM] * (len(parts) + 4),
        out_specs=[IN_VMEM] * 5,
        scratch_shapes=[
            pltpu.VMEM((TOKENS, LATE * LANE), jnp.bfloat16),
            pltpu.VMEM((4, TOKENS, LANE), jnp.float32),
        ],
        name="finish",
        cost_estimate=pl.CostEstimate(flops=2 * TOKENS * 768 * 512, bytes_accessed=5 << 20, transcendentals=0),
        compiler_params=pltpu.CompilerParams(vmem_limit_bytes=24 << 20),
    )(table, slots, *parts, gains, *begun)


def update_body(current, own, own_squares, *refs):
    arrived, result = refs[:3], refs[3]
    total, squares = own[...], own_squares[...]
    for ref in arrived:
        total = total + ref[0:TOKENS, :].astype(jnp.float32)
        tail = ref[TOKENS : TOKENS + TAIL, :].astype(jnp.float32)
        squares = squares + (tail[0:GROUPS] + tail[GROUPS : 2 * GROUPS] + tail[2 * GROUPS : 3 * GROUPS])
    scale = lax.rsqrt(squares * (1.0 / D) + EPSILON)
    column = jnp.concatenate(
        [jnp.broadcast_to(scale[a : a + 1], (LANE, LANE)).T for a in range(GROUPS)], axis=0
    )
    step = (total * column).astype(jnp.bfloat16).astype(jnp.float32)
    result[...] = (current[...].astype(jnp.float32) + step).astype(jnp.bfloat16)


def update(current, own, own_squares, arrived):
    return pl.pallas_call(
        update_body,
        out_shape=jax.ShapeDtypeStruct((TOKENS, LANE), jnp.bfloat16),
        in_specs=[IN_VMEM] * 6,
        out_specs=IN_VMEM,
        name="update",
        cost_estimate=pl.CostEstimate(flops=20 * TOKENS * LANE, bytes_accessed=1 << 20, transcendentals=512),
        compiler_params=pltpu.CompilerParams(vmem_limit_bytes=16 << 20),
    )(current, own, own_squares, *arrived)


def first_gram_body(table, kept, swapped, columns, result, turned, rows, arrived):
    @pl.when(table[20] == 1)
    def _():
        pltpu.make_async_copy(kept, rows, arrived).start()

    @pl.when(table[20] == 0)
    def _():
        pltpu.make_async_copy(swapped, rows, arrived).start()

    pltpu.make_async_copy(rows, rows, arrived).wait()
    right = columns[...]
    for b in range(NBLK):
        left = rows[b].T
        turned[b * LANE : (b + 1) * LANE, :] = left
        result[b] = jnp.dot(left, right, preferred_element_type=jnp.float32) * (1.0 / TOKENS)


def first_gram(table, kept, swapped, columns):
    return pl.pallas_call(
        first_gram_body,
        out_shape=[
            jax.ShapeDtypeStruct((NBLK, LANE, LANE), jnp.float32),
            jax.ShapeDtypeStruct((NBLK * LANE, TOKENS), jnp.bfloat16),
        ],
        in_specs=[IN_SMEM, IN_PLACE, IN_PLACE, IN_VMEM],
        out_specs=[IN_VMEM] * 2,
        scratch_shapes=[pltpu.VMEM((NBLK, TOKENS, LANE), jnp.bfloat16), pltpu.SemaphoreType.DMA],
        name="first_gram",
        cost_estimate=pl.CostEstimate(flops=2 * TOKENS * 2048 * LANE, bytes_accessed=5 << 20, transcendentals=0),
        compiler_params=pltpu.CompilerParams(vmem_limit_bytes=24 << 20),
    )(table, kept, swapped, columns)


def gram_body(turned, columns, result):
    total = jnp.dot(turned[...], columns[...], preferred_element_type=jnp.float32)
    result[...] = total.reshape(NBLK, LANE, LANE) * (1.0 / TOKENS)


def gram(turned, columns):
    return pl.pallas_call(
        gram_body,
        out_shape=jax.ShapeDtypeStruct((NBLK, LANE, LANE), jnp.float32),
        in_specs=[IN_VMEM] * 2,
        out_specs=IN_VMEM,
        name="gram",
        cost_estimate=pl.CostEstimate(flops=2 * TOKENS * 2048 * LANE, bytes_accessed=3 << 20, transcendentals=0),
        compiler_params=pltpu.CompilerParams(vmem_limit_bytes=16 << 20),
    )(turned, columns)


def to_other_core_of_chip(here):
    beside = send(here, ("y", "xl", "c"), (NY, 2, 2), lambda y, xl, c: (y, xl, 1 - c) if c == y % 2 else None)
    return jnp.where(lax.axis_index("c") == lax.axis_index("y") % 2, here, beside)


def quarter_of_section(block):
    own_quarter = 2 * lax.axis_index("xl") + lax.axis_index("c") == lax.axis_index("y")
    across = send(
        block, ("y", "xl", "c"), (NY, 2, 2), lambda y, xl, c: (y, 1 - xl, c) if 2 * xl + c == y else None
    )
    return to_other_core_of_chip(jnp.where(own_quarter, block, across))


def local(block_in, weights, gains, layer_counts):
    section = lax.axis_index("y")
    sections = jnp.arange(NY, dtype=jnp.int32)
    start = jnp.sum(jnp.where(sections < section, layer_counts, 0))
    layers = jnp.arange(LAYERS, dtype=jnp.int32)
    slots = jnp.clip(layers - start, 0, SLOTS - 1)
    ends = jnp.sum(jnp.where(sections[None, :] <= sections[:3, None], layer_counts[None, :], 0), axis=1)
    hops = jnp.any(ends[:, None] == layers[None, :] + 1, axis=0)
    table = lax.dynamic_index_in_dim(
        jnp.asarray(block_table()), lax.axis_index(("z", "xh", "xl", "c")), 0, keepdims=False
    )

    stays = lax.axis_index("xh") == lax.axis_index("c")
    by_block = block_in.transpose(1, 0, 2).reshape(TOKENS, LANE)
    mine = jnp.where(stays, by_block, swap_roles(by_block))
    gains = gains.reshape(SLOTS * NBLK, 1, LANE)
    gains = jnp.where(stays, gains, swap_roles(gains))

    def tile(slot, early, after):
        kept = finished_first(weights, early)[slot]
        return kept, swap_roles(finished_first(kept, after))

    other = other_core(mine)
    early = shared(first_round(mine, other))
    tiles = [tile(0, mine, other)]
    whole = assemble(table, early + second_round(early))
    current = lax.dynamic_index_in_dim(
        whole, 2 * lax.axis_index("z") + lax.axis_index("c"), 0, keepdims=False
    )
    turned = None
    for layer in range(LAYERS):
        if layer:
            other = other_core(current)
            matrix = fetch(layer, table, finished_first(slots, other), tiles)
            early = shared(first_round(current, other), matrix)
            begun = begin(
                layer, table, slots if turned is None else finished_first(slots, turned), early, gains, matrix
            )
            late = second_round(early, begun[1])
        else:
            matrix = fetch(layer, table, slots, tiles)
            early = late = [whole]
            begun = begin(layer, table, slots, early, gains, matrix)
        outs = finish(layer, table, slots, late, gains, [*begun, matrix])
        arrived = [along_x(outs[k], k + 1) for k in range(3)]
        current = update(current, outs[3], outs[4], arrived)
        if layer < SLOTS - 1:
            tiles.append(tile(layer + 1, outs[4], current))
        if layer == SLOTS:
            swapped = swap_roles(finished_first(whole, current))
        if layer == LAYERS - 2:
            at = 2 * lax.axis_index("z") + lax.axis_index("xh")
            x0 = jnp.where(
                stays,
                lax.dynamic_index_in_dim(whole, at, 0, keepdims=False),
                lax.dynamic_index_in_dim(swapped, at, 0, keepdims=False),
            )
            gram_in, turned = first_gram(table, whole, swapped, quarter_of_section(x0))
        if layer < LAYERS - 1:
            current = lax.cond(
                hops[layer],
                lambda v: send(v, ("y",), (NY,), lambda y: (y + 1,) if y < NY - 1 else None),
                lambda v: v,
                current,
            )

    def from_last(array, target):
        return send(
            array,
            ("xh", "y", "xl", "c"),
            (2, NY, 2, 2),
            lambda xh, y, xl, c: target(xh, xl, c) if y == NY - 1 else None,
        )

    by_tokens = lax.all_to_all(current.reshape(NBLK, TOKENS // NBLK, LANE), ("z", "c"), 0, 0, tiled=True)
    straight = from_last(current, lambda xh, xl, c: (c, 2 * xl + xh, xl, xh))
    across = from_last(current, lambda xh, xl, c: (c, 2 * xl + xh, 1 - xl, xh))
    own_quarter = 2 * lax.axis_index("xl") + lax.axis_index("c") == section
    gram_cross = gram(turned, to_other_core_of_chip(jnp.where(own_quarter, straight, across)))
    copies = [from_last(by_tokens, lambda xh, xl, c, plane=plane: (c, plane, xl, xh)) for plane in range(NY)]
    copies = finished_first(copies, gram_cross)
    block_out = copies[0]
    for plane in range(1, NY):
        block_out = jnp.where(section == plane, copies[plane], block_out)
    shape = (NBLK, LANE, 1, LANE)
    return block_out.transpose(1, 0, 2), gram_in.reshape(shape), gram_cross.reshape(shape)


def solution(mesh):
    finer = Mesh(mesh.devices.reshape(NZ, 2, NY, 2, 2), AXES)
    dp, section, tensor = ("z", "xh"), "y", ("xl", "c")
    return jax.shard_map(
        local,
        mesh=finer,
        in_specs=(P(dp, None, tensor), P(section, None, tensor, dp), P(section, None, tensor), P()),
        out_specs=(P(dp, None, tensor), P(None, tensor, dp, section), P(None, tensor, dp, section)),
        check_vma=False,
    )
```
